256 devices in a mesh: light: 16 (over y, x), depth: 16 (over z, core).
Axes of the slice: x: 4, y: 4, z: 8, core: 2. Of those that a mesh axis runs over, the one named last changes fastest.
Arguments:
- density: float32 [64, 512, 2048], P('light', None, 'depth'), may hold values from 0 to 1
- tf_table: float32 [8, 4, 4], replicated, may hold values from -4.5 to 11
- tf_index: int32 [16, 16], P('light', 'depth'), may hold values from 0 to 7
- light_sources: float32 [2, 512, 2048], P(None, None, 'depth'), may hold values from 0.25 to 2.5
- spread_taps: float32 [9], replicated, may hold values from 0.2 to 1
- view_flip: int32 [32768], P('light'), may hold values from 0 to 1
Outputs:
- image: float32 [4, 32768], P(None, ('light', 'depth'))
The draws below stay inside these ranges and needn't reach their ends.
All inputs are finite; a program needn't handle non-finite values.
Results may differ from the reference program's by a relative error of at most 0.0003.
Values sent between devices are 32-bit elements; how exact they have to be, the bound alone decides.
A program may use at most 64 MiB of HBM per device.

```python
import math
import jax
import jax.numpy as jnp
from jax import lax

LX = 4
WY = 512
CZ = 128
NTF = 8
DEG = 4
NX = 64
NZ = 2048
PIX = 32768
N_LIGHT = 16
N_DEPTH = 16


def draw_density(key, part):
    start_key = jax.random.fold_in(key, 11)
    base_key = jax.random.fold_in(key, 12)
    solid_key = jax.random.fold_in(key, 13)
    starts = jax.random.randint(start_key, (NX + 2, WY, NZ), 0, 1000, dtype=jnp.int32) < 15
    rod_cells = starts[2:] | starts[1:-1] | starts[:-2]
    lower_draw = jax.random.uniform(base_key, (NX, WY, NZ), jnp.float32)
    upper_draw = jax.random.uniform(solid_key, (NX, WY, NZ), jnp.float32)
    background = 0.4 * lower_draw
    solid_value = 0.85 + 0.15 * upper_draw
    return jnp.where(rod_cells, solid_value, background)


def draw_tf_table(key, part):
    color_key = jax.random.fold_in(key, 21)
    opacity_key = jax.random.fold_in(key, 22)
    colors = jnp.clip(1.5 * jax.random.normal(color_key, (NTF, 3, DEG), jnp.float32), -4.5, 4.5)
    uniforms = jax.random.uniform(opacity_key, (NTF, 4), jnp.float32)
    offset = -4.5 + 1.5 * uniforms[:, 0]
    linear = -0.5 + uniforms[:, 1]
    square_term = -0.5 + uniforms[:, 2]
    cubic = 8.0 + 3.0 * uniforms[:, 3]
    opacity_row = jnp.stack([offset, linear, square_term, cubic], axis=1)[:, None, :]
    return jnp.concatenate([colors, opacity_row], axis=1)


def place_ends(entries, key, smallest, largest):
    spot = [jax.random.randint(jax.random.fold_in(key, axis), (), 0, length) for axis, length in enumerate(entries.shape)]
    main_axis = entries.shape.index(max(entries.shape))
    neighbour = spot[:main_axis] + [(spot[main_axis] + 1) % entries.shape[main_axis]] + spot[main_axis + 1:]
    return entries.at[tuple(spot)].set(smallest).at[tuple(neighbour)].set(largest)


def steps_of(rng, dims, pieces, smallest, largest):
    gain = 1.0
    for axis_at, blocks in pieces:
        draws = jax.random.uniform(jax.random.fold_in(jax.random.fold_in(rng, 6), axis_at), (blocks,), jnp.float32, smallest / len(pieces), largest / len(pieces))
        gain = gain * jnp.repeat(jnp.exp(draws), dims[axis_at] // blocks).reshape((-1,) + (1,) * (len(dims) - 1 - axis_at))
    return gain


def setup_inputs(seed: int = 0) -> dict:
    seeds = jax.random.split(jax.random.key(seed), 7)
    density = draw_density(jax.random.fold_in(seeds[6], 71), 0)
    tf_table = draw_tf_table(jax.random.fold_in(seeds[6], 71), 0)
    tf_index = place_ends(jax.random.randint(seeds[2], (N_LIGHT, N_DEPTH), 0, NTF), jax.random.fold_in(seeds[2], 1), 0, NTF - 1).astype(jnp.int32)
    light_sources = jnp.clip(jnp.exp(math.log(2.5) - 2.3025851 * jax.random.uniform(seeds[3], (2, WY, NZ), jnp.float32) ** steps_of(seeds[3], (2, WY, NZ), ((2, 16),), -0.2, 0.2)), 0.25, 2.5)
    spread_taps = jnp.clip(jnp.exp(jax.random.uniform(seeds[4], (9,), jnp.float32, math.log(0.2), math.log(1.0))), 0.2, 1.0)
    view_flip = place_ends(jax.random.randint(seeds[5], (PIX,), 0, 2), jax.random.fold_in(seeds[5], 1), 0, 1).astype(jnp.int32)
    return dict(density=density, tf_table=tf_table, tf_index=tf_index, light_sources=light_sources, spread_taps=spread_taps, view_flip=view_flip)


AMBIENT = 0.2
LIGHT_DEPTH = 36.0
VIEW_DEPTH = 16.0


def spread(plane, weights):
    lead = [(0, 0)] * (plane.ndim - 2)
    rows = plane.shape[-2]
    padded = jnp.pad(plane, lead + [(4, 4), (0, 0)])
    across = weights[0] * padded[..., 0:rows, :]
    for tap in range(1, 9):
        across = across + weights[tap] * padded[..., tap:tap + rows, :]
    cols = plane.shape[-1]
    padded = jnp.pad(across, lead + [(0, 0), (4, 4)])
    result = weights[0] * padded[..., 0:cols]
    for tap in range(1, 9):
        result = result + weights[tap] * padded[..., tap:tap + cols]
    return result


def channel(values, coefs):
    return jax.nn.sigmoid(((coefs[3] * values + coefs[2]) * values + coefs[1]) * values + coefs[0])


def reference(density, tf_table, tf_index, light_sources, spread_taps, view_flip):
    weights = spread_taps / jnp.sum(spread_taps)
    dens_slabs = density.reshape(N_LIGHT, LX, WY, N_DEPTH, CZ)
    brick_coefs = tf_table[tf_index]

    def slab_channel(args, kind):
        slab, coefs = args
        per = [coefs[:, kind, k][None, None, :, None] for k in range(DEG)]
        return channel(slab, per)

    opacity = lax.map(lambda a: slab_channel(a, 3), (dens_slabs, brick_coefs)).reshape(NX, WY, NZ)
    absorb = LIGHT_DEPTH / NX

    def advance(buf, slice_opacity):
        return spread(buf, weights) * jnp.exp(-absorb * slice_opacity), buf

    _, forward = lax.scan(advance, light_sources[0], opacity)
    _, backward = lax.scan(advance, light_sources[1], opacity, reverse=True)
    lit_slabs = (AMBIENT + forward + backward).reshape(N_LIGHT, LX, WY, NZ)
    opac_slabs = opacity.reshape(N_LIGHT, LX, WY, NZ)
    flip_slabs = (view_flip != 0).reshape(N_LIGHT, LX, WY, 1)

    def shade(args):
        slab, coefs, lit, opac, flip = args
        tau = (VIEW_DEPTH / NZ) * opac
        cum = jnp.cumsum(tau, axis=-1)
        total = cum[..., -1:]
        before = jnp.where(flip, total - cum, cum - tau)
        trans = jnp.exp(-before) * lit * (1.0 - jnp.exp(-tau))
        planes = []
        for kind in range(3):
            per = [coefs[:, kind, k][None, None, :, None] for k in range(DEG)]
            color = channel(slab, per).reshape(LX, WY, NZ)
            planes.append(jnp.sum(trans * color, axis=-1).reshape(LX * WY))
        planes.append((1.0 - jnp.exp(-total[..., 0])).reshape(LX * WY))
        return jnp.stack(planes)

    images = lax.map(shade, (dens_slabs, brick_coefs, lit_slabs, opac_slabs, flip_slabs))
    return jnp.transpose(images, (1, 0, 2)).reshape(4, PIX)
```

```python
import functools

import jax
import jax.numpy as jnp
from jax import lax
from jax.experimental import pallas as pl
from jax.experimental.pallas import tpu as pltpu
from jax.sharding import PartitionSpec as P

AMBIENT = 0.2
LIGHT_DEPTH = 36.0
VIEW_DEPTH = 16.0

SL = 4
ROWS = 512
LANES = 128
CH = 32
NCH = 17
PAD = 32
TALL = PAD + NCH * CH
FCH = 64
NF = ROWS // FCH
BLOCKS = SL * ROWS // LANES
MESH = pl.DeviceIdType.MESH


def channel(v, c):
    return jax.nn.sigmoid(((c[3] * v + c[2]) * v + c[1]) * v + c[0])


def kernel(
    nl,
    nd,
    dens,
    table,
    index,
    sources,
    taps,
    flips,
    out,
    lev,
    leave,
    fade,
    fade_nb,
    light_nb,
    weight,
    totals,
    gathered,
    part,
    parts,
    s_main,
    r_main,
    s_nb,
    r_nb,
    s_fade,
    r_fade,
    s_tot,
    r_tot,
    s_part,
    r_part,
):
    l = lax.axis_index("light")
    d = lax.axis_index("depth")
    has_left = d > 0
    has_right = d < nd - 1
    mine = BLOCKS // nd
    f32 = jnp.float32

    zeros = jnp.zeros((PAD, LANES), f32)
    for way in range(2):
        for s in range(SL):
            for tile in range(2):
                lev[way, s, tile, 0:PAD, :] = zeros
        for tile in range(2):
            lev[way, 0, tile, PAD + ROWS : TALL, :] = zeros
    for x in range(SL):
        fade[x, 0:PAD, :] = zeros
        fade[x, PAD + ROWS : TALL, :] = zeros
        for side in range(2):
            fade_nb[side, x, 0:PAD, :] = zeros
            fade_nb[side, x, PAD + ROWS : TALL, :] = zeros
    for side, there in ((0, has_left), (1, has_right)):

        @pl.when(jnp.logical_not(there))
        def _():
            @pl.loop(0, ROWS // CH)
            def _(i):
                at = pl.ds(pl.multiple_of(PAD + i * CH, CH), CH)
                for x in range(SL):
                    fade_nb[side, x, at, :] = zeros
                for way in range(2):
                    light_nb[way, side, at, :] = zeros

    for way, first in ((0, 0), (1, nl - 1)):

        @pl.when(l == first)
        def _():
            @pl.loop(0, ROWS // CH)
            def _(i):
                lev[way, 0, 0, pl.ds(pl.multiple_of(PAD + i * CH, CH), CH), :] = sources[
                    way, pl.ds(pl.multiple_of(i * CH, CH), CH), :
                ]

    barrier = pltpu.get_barrier_semaphore()

    def greet(to_l, to_d):
        pl.semaphore_signal(barrier, 1, device_id=(to_l, to_d), device_id_type=MESH)

    @pl.loop(1, nd)
    def _(j):
        greet(l, lax.rem(d + j, nd))

    for dl in (-1, 1):
        near = (l + dl >= 0) & (l + dl < nl)
        for dd in (-1, 0, 1):

            @pl.when(near & (d + dd >= 0) & (d + dd < nd))
            def _():
                greet(l + dl, d + dd)

    k_at = index[0, 0]
    coef = [[table[k_at, k, j] for j in range(4)] for k in range(4)]
    absorb = LIGHT_DEPTH / (SL * nl)
    thick = VIEW_DEPTH / (nd * LANES)

    @pl.loop(0, NF)
    def _(i):
        src = pl.ds(pl.multiple_of(i * FCH, FCH), FCH)
        dst = pl.ds(pl.multiple_of(PAD + i * FCH, 32), FCH)
        for x in range(SL):
            fade[x, dst, :] = jnp.exp(-absorb * channel(dens[x, src, :], coef[3]))

    beside = (has_left.astype(jnp.int32) + has_right.astype(jnp.int32)) + 1
    lights = (l > 0).astype(jnp.int32) + (l < nl - 1).astype(jnp.int32)
    pl.semaphore_wait(barrier, nd - 1 + lights * beside)

    def fade_copy(side, i):
        rows = pl.ds(pl.multiple_of(PAD + i * FCH, 32), FCH)
        to = d - 1 + 2 * side
        return pltpu.make_async_remote_copy(
            src_ref=fade.at[:, rows, :],
            dst_ref=fade_nb.at[1 - side, :, rows, :],
            send_sem=s_fade.at[side, i],
            recv_sem=r_fade.at[1 - side, i],
            device_id=(l, to),
            device_id_type=MESH,
        )

    def source_copy(way, side, j):
        return pltpu.make_async_remote_copy(
            src_ref=sources.at[way, pl.ds(pl.multiple_of(j * CH, CH), CH), :],
            dst_ref=light_nb.at[way, 1 - side, pl.ds(pl.multiple_of(PAD + j * CH, CH), CH), :],
            send_sem=s_nb.at[way, side, j],
            recv_sem=r_nb.at[way, 1 - side, j],
            device_id=(l, d - 1 + 2 * side),
            device_id_type=MESH,
        )

    sides = ((0, has_left), (1, has_right))

    @pl.loop(0, NF)
    def _(i):
        for side, there in sides:
            for way, first in ((0, 0), (1, nl - 1)):

                @pl.when(there & (l == first))
                def _():
                    source_copy(way, side, 2 * i).start()
                    source_copy(way, side, 2 * i + 1).start()

            @pl.when(there)
            def _():
                fade_copy(side, i).start()

    total_tap = taps[0]
    for t in range(1, 9):
        total_tap = total_tap + taps[t]
    total_vec = jnp.full((8, LANES), total_tap, f32)
    tap = [(jnp.full((8, LANES), taps[t], f32) / total_vec)[0:1, :] for t in range(9)]
    lane = lax.broadcasted_iota(jnp.int32, (CH, LANES), 1)
    low_half = lane < LANES // 2

    def hops(way):
        return l + way * (nl - 1 - 2 * l)

    def rows_out(way, i):
        n = hops(way)
        return pl.ds(pl.multiple_of(PAD - 16 + i * CH - 16 * lax.rem(n, 2), 16), CH)

    def main_copy(way, i):
        rows = rows_out(way, i)
        return pltpu.make_async_remote_copy(
            src_ref=leave.at[way, :, rows, :],
            dst_ref=lev.at[way, 0, :, rows, :],
            send_sem=s_main.at[way, i],
            recv_sem=r_main.at[way, i - lax.rem(hops(way), 2)],
            device_id=(l + 1 - 2 * way, d),
            device_id_type=MESH,
        )

    def side_copy(way, side, i):
        rows = rows_out(way, i)
        return pltpu.make_async_remote_copy(
            src_ref=leave.at[way, 0, rows, :],
            dst_ref=light_nb.at[way, 1 - side, rows, :],
            send_sem=s_nb.at[way, side, i],
            recv_sem=r_nb.at[way, 1 - side, i - 1],
            device_id=(l + 1 - 2 * way, d - 1 + 2 * side),
            device_id_type=MESH,
        )

    def wait_recv(dst, sem):
        pltpu.make_async_copy(dst, dst, sem).wait()

    def step(way, i, lead):
        n = hops(way)
        odd = lax.rem(n, 2)
        base = pl.multiple_of(PAD + i * CH - 16 * odd, 16)
        rows = pl.ds(base, CH)

        for side, there in sides:

            @pl.when(there & lead & (lax.rem(i, 2) == 0) & (i < 2 * NF))
            def _():
                at = pl.ds(pl.multiple_of(PAD + i * CH, CH), FCH)
                wait_recv(fade_nb.at[side, :, at, :], r_fade.at[side, lax.div(i, 2)])

        @pl.when((n > 0) & (i < NCH - 1 + odd))
        def _():
            wait_recv(lev.at[way, 0, :, rows, :], r_main.at[way, i])

        @pl.when((lax.rem(n, 4) == 0) & (i < NCH - 1))
        def _():
            for side, there in sides:

                @pl.when(there)
                def _():
                    wait_recv(light_nb.at[way, side, rows, :], r_nb.at[way, side, i])

            lev[way, 0, 1, rows, :] = jnp.where(
                low_half, light_nb[way, 1, rows, :], light_nb[way, 0, rows, :]
            )

        for s in range(SL):
            layer = s + way * (SL - 1 - 2 * s)
            cols = []
            for tile in range(2):
                acc = tap[0] * lev[way, s, tile, pl.ds(base - 8, CH), :]
                for t in range(1, 9):
                    acc = acc + tap[t] * lev[way, s, tile, pl.ds(base - 8 + t, CH), :]
                cols.append(acc)
            a, b = cols
            sum_a, sum_b = tap[4] * a, tap[4] * b
            for t in range(9):
                by = t - 4
                if by == 0:
                    continue
                ra = pltpu.roll(a, (-by) % LANES, 1)
                rb = pltpu.roll(b, (-by) % LANES, 1)
                own = lane < LANES - by if by > 0 else lane >= -by
                sum_a = sum_a + tap[t] * jnp.where(own, ra, rb)
                sum_b = sum_b + tap[t] * jnp.where(own, rb, ra)
            there_rows = pl.ds(base - 4 * (s + 1), CH)
            fade_a = fade[layer, there_rows, :]
            fade_b = jnp.where(
                low_half, fade_nb[1, layer, there_rows, :], fade_nb[0, layer, there_rows, :]
            )
            if s < SL - 1:
                lev[way, s + 1, 0, rows, :] = sum_a * fade_a
                lev[way, s + 1, 1, rows, :] = sum_b * fade_b
            else:
                leave[way, 0, rows_out(way, i), :] = sum_a * fade_a
                leave[way, 1, rows_out(way, i), :] = sum_b * fade_b

        @pl.when((n < nl - 1) & (i >= odd))
        def _():
            main_copy(way, i).start()
            for side, there in sides:

                @pl.when(there & (lax.rem(n, 4) == 3))
                def _():
                    side_copy(way, side, i).start()

    row_i = lax.broadcasted_iota(jnp.int32, (LANES, LANES), 0)
    lane_i = lax.broadcasted_iota(jnp.int32, (LANES, LANES), 1)

    def compact(column):
        return jnp.sum(jnp.where(row_i == lane_i, column, 0.0), axis=0, keepdims=True)

    def total_copy(j):
        peer = lax.rem(d + j, nd)
        return pltpu.make_async_remote_copy(
            src_ref=totals,
            dst_ref=gathered.at[d],
            send_sem=s_tot.at[j],
            recv_sem=r_tot.at[d],
            device_id=(l, peer),
            device_id_type=MESH,
        )

    def prepare():
        earlier = (row_i < lane_i).astype(f32)
        later = (row_i > lane_i).astype(f32)

        @pl.loop(0, BLOCKS)
        def _(b):
            x = lax.div(b, SL)
            at = pl.ds(pl.multiple_of(lax.rem(b, SL) * LANES, LANES), LANES)
            v = dens[x, at, :]
            tau = thick * channel(v, coef[3])
            front = jnp.dot(tau, earlier, precision=lax.Precision.HIGHEST, preferred_element_type=f32)
            back = jnp.dot(tau, later, precision=lax.Precision.HIGHEST, preferred_element_type=f32)
            flip = jnp.broadcast_to(flips[pl.ds(b, 1), :].astype(f32), (LANES, LANES)).T
            before = jnp.where(flip != 0.0, back, front)
            common = jnp.exp(-before) * (1.0 - jnp.exp(-tau))
            for k in range(3):
                weight[k, x, at, :] = common * channel(v, coef[k])
            totals[pl.ds(b, 1), :] = compact(jnp.sum(tau, axis=1, keepdims=True))

        @pl.loop(1, nd)
        def _(j):
            total_copy(j).start()

    lead_way = (2 * l >= nl).astype(jnp.int32)
    n_lead = hops(lead_way)
    gap = jnp.where(2 * n_lead >= nl - 2, 5, NCH)
    prep_at = jnp.where(n_lead >= 4, 0, NCH)

    @pl.loop(0, 2 * NCH + 1)
    def _(item):
        @pl.when(item == prep_at)
        def _():
            prepare()

        @pl.when(item != prep_at)
        def _():
            k = item - (item > prep_at).astype(jnp.int32)
            both = NCH - gap
            e = k - gap
            mixed = (e >= 0) & (e < 2 * both)
            is_lead = (e < 0) | (mixed & (lax.rem(e + 2 * NCH, 2) == 0))
            half = lax.div(e + 2 * NCH, 2) - NCH
            i = jnp.where(e < 0, k, jnp.where(mixed, jnp.where(is_lead, gap + half, half), e - both))
            way = jnp.where(is_lead, lead_way, 1 - lead_way)
            step(way, i, is_lead)

    @pl.loop(1, nd)
    def _(j):
        peer = lax.rem(d + j, nd)
        wait_recv(gathered.at[peer], r_tot.at[peer])

    gathered[d] = totals[...]
    flip_px = flips[...] != 0
    offset = jnp.zeros((BLOCKS, LANES), f32)
    whole = jnp.zeros((BLOCKS, LANES), f32)
    for src in range(nd):
        got = gathered[src]
        whole = whole + got
        ahead = jnp.where(flip_px, src - d, d - src) > 0
        offset = offset + jnp.where(ahead, got, 0.0)
    through = jnp.exp(-offset)
    totals_scaled = 1.0 - jnp.exp(-whole)

    for b in range(BLOCKS):
        x = b // SL
        y = (b % SL) * LANES
        fwd = lev[0, x, 0, PAD + y + 4 * x : PAD + y + 4 * x + LANES, :]
        z = SL - 1 - x
        bwd = lev[1, z, 0, PAD + y + 4 * z : PAD + y + 4 * z + LANES, :]
        lit = AMBIENT + fwd + bwd
        for k in range(3):
            s = jnp.sum(weight[k, x, y : y + LANES, :] * lit, axis=1, keepdims=True)
            part[b, k : k + 1, :] = compact(s) * through[b : b + 1, :]
        part[b, 3:4, :] = totals_scaled[b : b + 1, :]

    def part_copy(j):
        peer = lax.rem(d + j, nd)
        return pltpu.make_async_remote_copy(
            src_ref=part.at[pl.ds(peer * mine, mine)],
            dst_ref=parts.at[d],
            send_sem=s_part.at[j],
            recv_sem=r_part.at[d],
            device_id=(l, peer),
            device_id_type=MESH,
        )

    @pl.loop(1, nd)
    def _(j):
        part_copy(j).start()

    own = part[pl.ds(d * mine, mine)]
    image = own

    @pl.loop(1, nd)
    def _(j):
        peer = lax.rem(d + j, nd)
        wait_recv(parts.at[peer], r_part.at[peer])

    parts[d] = own
    image = parts[0]
    for src in range(1, nd):
        image = image + parts[src]
    for m in range(mine):
        at = slice(m * LANES, (m + 1) * LANES)
        out[0:3, at] = image[m, 0:3, :]
        out[3:4, at] = own[m, 3:4, :]

    @pl.loop(1, nd)
    def _(j):
        total_copy(j).wait_send()
        part_copy(j).wait_send()

    for side, there in sides:

        @pl.when(there)
        def _():
            @pl.loop(0, NF)
            def _(i):
                fade_copy(side, i).wait_send()

    for way, first in ((0, 0), (1, nl - 1)):
        n = hops(way)
        odd = lax.rem(n, 2)

        @pl.loop(0, NCH)
        def _(i):
            @pl.when((n < nl - 1) & (i >= odd))
            def _():
                main_copy(way, i).wait_send()

            for side, there in sides:

                @pl.when(there & (n < nl - 1) & (lax.rem(n, 4) == 3) & (i >= odd))
                def _():
                    side_copy(way, side, i).wait_send()

                @pl.when(there & (l == first) & (i < NCH - 1))
                def _():
                    source_copy(way, side, i).wait_send()


def solution(mesh):
    nl, nd = mesh.shape["light"], mesh.shape["depth"]
    mine = BLOCKS // nd
    f32 = jnp.float32
    dma = pltpu.SemaphoreType.DMA

    def per_device(density, tf_table, tf_index, light_sources, spread_taps, view_flip):
        vmem = pl.BlockSpec(memory_space=pltpu.VMEM)
        smem = pl.BlockSpec(memory_space=pltpu.SMEM)
        return pl.pallas_call(
            functools.partial(kernel, nl, nd),
            out_shape=jax.ShapeDtypeStruct((4, mine * LANES), f32),
            in_specs=[vmem, smem, smem, vmem, smem, vmem],
            out_specs=vmem,
            scratch_shapes=[
                pltpu.VMEM((2, SL, 2, TALL, LANES), f32),
                pltpu.VMEM((2, 2, TALL, LANES), f32),
                pltpu.VMEM((SL, TALL, LANES), f32),
                pltpu.VMEM((2, SL, TALL, LANES), f32),
                pltpu.VMEM((2, 2, TALL, LANES), f32),
                pltpu.VMEM((3, SL, ROWS, LANES), f32),
                pltpu.VMEM((BLOCKS, LANES), f32),
                pltpu.VMEM((nd, BLOCKS, LANES), f32),
                pltpu.VMEM((BLOCKS, 8, LANES), f32),
                pltpu.VMEM((nd, mine, 8, LANES), f32),
                dma((2, NCH)),
                dma((2, NCH)),
                dma((2, 2, NCH)),
                dma((2, 2, NCH)),
                dma((2, NF)),
                dma((2, NF)),
                dma((nd,)),
                dma((nd,)),
                dma((nd,)),
                dma((nd,)),
            ],
            compiler_params=pltpu.CompilerParams(
                collective_id=0, has_side_effects=True, vmem_limit_bytes=48 << 20
            ),
            name="waves",
        )(density, tf_table, tf_index, light_sources, spread_taps, view_flip.reshape(BLOCKS, LANES))

    return jax.shard_map(
        per_device,
        mesh=mesh,
        in_specs=(
            P("light", None, "depth"),
            P(),
            P("light", "depth"),
            P(None, None, "depth"),
            P(),
            P("light"),
        ),
        out_specs=P(None, ("light", "depth")),
        check_vma=False,
    )
```

```python
import functools

import jax
import jax.numpy as jnp
from jax import lax
from jax.experimental import pallas as pl
from jax.experimental.pallas import tpu as pltpu
from jax.sharding import PartitionSpec as P

AMBIENT = 0.2
LIGHT_DEPTH = 36.0
VIEW_DEPTH = 16.0

SL = 4
ROWS = 512
LANES = 128
CH = 32
NCH = 17
PAD = 32
TALL = PAD + NCH * CH
FCH = 64
NF = ROWS // FCH
BLOCKS = SL * ROWS // LANES
MESH = pl.DeviceIdType.MESH


def channel(v, c):
    return jax.nn.sigmoid(((c[3] * v + c[2]) * v + c[1]) * v + c[0])


def kernel(
    nl,
    nd,
    dens,
    table,
    index,
    sources,
    taps,
    flips,
    out,
    lev,
    outbox,
    inbox,
    side_out,
    side_in,
    fade,
    fade_nb,
    light_nb,
    weight,
    totals,
    gathered,
    part,
    parts,
    s_main,
    r_main,
    s_nb,
    r_nb,
    s_fade,
    r_fade,
    s_tot,
    r_tot,
    s_part,
    r_part,
):
    l = lax.axis_index("light")
    d = lax.axis_index("depth")
    has_left = d > 0
    has_right = d < nd - 1
    mine = BLOCKS // nd
    f32 = jnp.float32

    zeros = jnp.zeros((PAD, LANES), f32)
    for way in range(2):
        for s in range(SL):
            for tile in range(2):
                lev[way, s, tile, 0:PAD, :] = zeros
        for tile in range(2):
            lev[way, 0, tile, PAD + ROWS : TALL, :] = zeros
    for x in range(SL):
        fade[x, 0:PAD, :] = zeros
        fade[x, PAD + ROWS : TALL, :] = zeros
        for side in range(2):
            fade_nb[side, x, 0:PAD, :] = zeros
            fade_nb[side, x, PAD + ROWS : TALL, :] = zeros
    for side, there in ((0, has_left), (1, has_right)):

        @pl.when(jnp.logical_not(there))
        def _():
            @pl.loop(0, ROWS // CH)
            def _(i):
                at = pl.ds(pl.multiple_of(PAD + i * CH, CH), CH)
                for x in range(SL):
                    fade_nb[side, x, at, :] = zeros
                for way in range(2):
                    light_nb[way, side, at, :] = zeros
                    side_in[way, side, i, :, :] = zeros[0 : CH // 2]

    for way, first in ((0, 0), (1, nl - 1)):

        @pl.when(l == first)
        def _():
            @pl.loop(0, ROWS // CH)
            def _(i):
                lev[way, 0, 0, pl.ds(pl.multiple_of(PAD + i * CH, CH), CH), :] = sources[
                    way, pl.ds(pl.multiple_of(i * CH, CH), CH), :
                ]

    barrier = pltpu.get_barrier_semaphore()

    def greet(to_l, to_d):
        pl.semaphore_signal(barrier, 1, device_id=(to_l, to_d), device_id_type=MESH)

    @pl.loop(1, nd)
    def _(j):
        greet(l, lax.rem(d + j, nd))

    for dl in (-1, 1):
        near = (l + dl >= 0) & (l + dl < nl)
        for dd in (-1, 0, 1):

            @pl.when(near & (d + dd >= 0) & (d + dd < nd))
            def _():
                greet(l + dl, d + dd)

    k_at = index[0, 0]
    coef = [[table[k_at, k, j] for j in range(4)] for k in range(4)]
    absorb = LIGHT_DEPTH / (SL * nl)
    thick = VIEW_DEPTH / (nd * LANES)

    @pl.loop(0, NF)
    def _(i):
        src = pl.ds(pl.multiple_of(i * FCH, FCH), FCH)
        dst = pl.ds(pl.multiple_of(PAD + i * FCH, 32), FCH)
        for x in range(SL):
            fade[x, dst, :] = jnp.exp(-absorb * channel(dens[x, src, :], coef[3]))

    beside = (has_left.astype(jnp.int32) + has_right.astype(jnp.int32)) + 1
    lights = (l > 0).astype(jnp.int32) + (l < nl - 1).astype(jnp.int32)
    pl.semaphore_wait(barrier, nd - 1 + lights * beside)

    def fade_copy(side, i):
        rows = pl.ds(pl.multiple_of(PAD + i * FCH, 32), FCH)
        to = d - 1 + 2 * side
        return pltpu.make_async_remote_copy(
            src_ref=fade.at[:, rows, :],
            dst_ref=fade_nb.at[1 - side, :, rows, :],
            send_sem=s_fade.at[side, i],
            recv_sem=r_fade.at[1 - side, i],
            device_id=(l, to),
            device_id_type=MESH,
        )

    def source_copy(way, side, j):
        return pltpu.make_async_remote_copy(
            src_ref=sources.at[way, pl.ds(pl.multiple_of(j * CH, CH), CH), :],
            dst_ref=light_nb.at[way, 1 - side, pl.ds(pl.multiple_of(PAD + j * CH, CH), CH), :],
            send_sem=s_nb.at[way, side, j],
            recv_sem=r_nb.at[way, 1 - side, j],
            device_id=(l, d - 1 + 2 * side),
            device_id_type=MESH,
        )

    sides = ((0, has_left), (1, has_right))

    @pl.loop(0, NF)
    def _(i):
        for side, there in sides:
            for way, first in ((0, 0), (1, nl - 1)):

                @pl.when(there & (l == first))
                def _():
                    source_copy(way, side, 2 * i).start()
                    source_copy(way, side, 2 * i + 1).start()

            @pl.when(there)
            def _():
                fade_copy(side, i).start()

    total_tap = taps[0]
    for t in range(1, 9):
        total_tap = total_tap + taps[t]
    total_vec = jnp.full((8, LANES), total_tap, f32)
    tap = [(jnp.full((8, LANES), taps[t], f32) / total_vec)[0:1, :] for t in range(9)]
    lane = lax.broadcasted_iota(jnp.int32, (CH, LANES), 1)
    low_half = lane < LANES // 2
    half_ch = CH // 2

    def hops(way):
        return l + way * (nl - 1 - 2 * l)

    def sizes(n):
        m = lax.rem(n, 4)
        return ((CH, m == 3), (2 * CH, m == 0), (CH + CH // 2, (m == 1) | (m == 2)))

    def main_copy(way, i, size):
        return pltpu.make_async_remote_copy(
            src_ref=outbox.at[way, i, pl.ds(0, size), :],
            dst_ref=inbox.at[way, i - lax.rem(hops(way), 2), pl.ds(0, size), :],
            send_sem=s_main.at[way, i],
            recv_sem=r_main.at[way, i - lax.rem(hops(way), 2)],
            device_id=(l + 1 - 2 * way, d),
            device_id_type=MESH,
        )

    def side_copy(way, side, i):
        return pltpu.make_async_remote_copy(
            src_ref=side_out.at[way, side, i],
            dst_ref=side_in.at[way, 1 - side, i - 1],
            send_sem=s_nb.at[way, side, i],
            recv_sem=r_nb.at[way, 1 - side, i - 1],
            device_id=(l + 1 - 2 * way, d - 1 + 2 * side),
            device_id_type=MESH,
        )

    def wait_recv(dst, sem):
        pltpu.make_async_copy(dst, dst, sem).wait()

    def step(way, i, lead):
        n = hops(way)
        odd = lax.rem(n, 2)
        base = pl.multiple_of(PAD + i * CH - 16 * odd, 16)
        rows = pl.ds(base, CH)

        for side, there in sides:

            @pl.when(there & lead & (lax.rem(i, 2) == 0) & (i < 2 * NF))
            def _():
                at = pl.ds(pl.multiple_of(PAD + i * CH, CH), FCH)
                wait_recv(fade_nb.at[side, :, at, :], r_fade.at[side, lax.div(i, 2)])

        for size, sent in sizes(n + 3):

            @pl.when((n > 0) & sent & (i < NCH - 1 + odd))
            def _():
                wait_recv(inbox.at[way, i, pl.ds(0, size), :], r_main.at[way, i])
                lev[way, 0, 0, rows, :] = inbox[way, i, 0:CH, :]
                if size == 2 * CH:
                    lev[way, 0, 1, rows, :] = inbox[way, i, CH : 2 * CH, :]
                elif size > CH:
                    near = inbox[way, i, CH:size, :]
                    lev[way, 0, 1, pl.ds(base, half_ch), :] = pltpu.roll(near, 96, 1)
                    lev[way, 0, 1, pl.ds(base + half_ch, half_ch), :] = pltpu.roll(near, 32, 1)

        @pl.when((lax.rem(n, 4) == 0) & (i < NCH - 1))
        def _():
            @pl.when(n == 0)
            def _():
                for side, there in sides:

                    @pl.when(there)
                    def _():
                        wait_recv(light_nb.at[way, side, rows, :], r_nb.at[way, side, i])

                lev[way, 0, 1, rows, :] = jnp.where(
                    low_half, light_nb[way, 1, rows, :], light_nb[way, 0, rows, :]
                )

            @pl.when(n > 0)
            def _():
                for side, there in sides:

                    @pl.when(there)
                    def _():
                        wait_recv(side_in.at[way, side, i], r_nb.at[way, side, i])

                lo = side_in[way, 0, i]
                hi = side_in[way, 1, i]
                low = low_half[0:half_ch]
                lev[way, 0, 1, pl.ds(base, half_ch), :] = jnp.where(
                    low, hi, pltpu.roll(lo, LANES // 2, 1)
                )
                lev[way, 0, 1, pl.ds(base + half_ch, half_ch), :] = jnp.where(
                    low, pltpu.roll(hi, LANES // 2, 1), lo
                )

        for s in range(SL):
            layer = s + way * (SL - 1 - 2 * s)
            cols = []
            for tile in range(2):
                acc = tap[0] * lev[way, s, tile, pl.ds(base - 8, CH), :]
                for t in range(1, 9):
                    acc = acc + tap[t] * lev[way, s, tile, pl.ds(base - 8 + t, CH), :]
                cols.append(acc)
            a, b = cols
            sum_a, sum_b = tap[4] * a, tap[4] * b
            for t in range(9):
                by = t - 4
                if by == 0:
                    continue
                ra = pltpu.roll(a, (-by) % LANES, 1)
                rb = pltpu.roll(b, (-by) % LANES, 1)
                own = lane < LANES - by if by > 0 else lane >= -by
                sum_a = sum_a + tap[t] * jnp.where(own, ra, rb)
                sum_b = sum_b + tap[t] * jnp.where(own, rb, ra)
            there_rows = pl.ds(base - 4 * (s + 1), CH)
            fade_a = fade[layer, there_rows, :]
            fade_b = jnp.where(
                low_half, fade_nb[1, layer, there_rows, :], fade_nb[0, layer, there_rows, :]
            )
            if s < SL - 1:
                lev[way, s + 1, 0, rows, :] = sum_a * fade_a
                lev[way, s + 1, 1, rows, :] = sum_b * fade_b
            else:
                last_a, last_b = sum_a * fade_a, sum_b * fade_b

        for size, sent in sizes(n):

            @pl.when((n < nl - 1) & sent & (i >= odd))
            def _():
                outbox[way, i, 0:CH, :] = last_a
                low = low_half[0:half_ch]
                if size == 2 * CH:
                    outbox[way, i, CH : 2 * CH, :] = last_b
                elif size > CH:
                    outbox[way, i, CH:size, :] = jnp.where(
                        low, pltpu.roll(last_b[0:half_ch], 32, 1), pltpu.roll(last_b[half_ch:CH], 96, 1)
                    )
                main_copy(way, i, size).start()
                if size == CH:
                    top, bottom = last_a[0:half_ch], last_a[half_ch:CH]
                    side_out[way, 0, i] = jnp.where(low, top, pltpu.roll(bottom, LANES // 2, 1))
                    side_out[way, 1, i] = jnp.where(low, pltpu.roll(top, LANES // 2, 1), bottom)
                    for side, there in sides:

                        @pl.when(there)
                        def _():
                            side_copy(way, side, i).start()

    row_i = lax.broadcasted_iota(jnp.int32, (LANES, LANES), 0)
    lane_i = lax.broadcasted_iota(jnp.int32, (LANES, LANES), 1)

    def compact(column):
        return jnp.sum(jnp.where(row_i == lane_i, column, 0.0), axis=0, keepdims=True)

    def total_copy(j):
        peer = lax.rem(d + j, nd)
        return pltpu.make_async_remote_copy(
            src_ref=totals,
            dst_ref=gathered.at[d],
            send_sem=s_tot.at[j],
            recv_sem=r_tot.at[d],
            device_id=(l, peer),
            device_id_type=MESH,
        )

    def prepare():
        earlier = (row_i < lane_i).astype(f32)
        later = (row_i > lane_i).astype(f32)

        @pl.loop(0, BLOCKS)
        def _(b):
            x = lax.div(b, SL)
            at = pl.ds(pl.multiple_of(lax.rem(b, SL) * LANES, LANES), LANES)
            v = dens[x, at, :]
            tau = thick * channel(v, coef[3])
            front = jnp.dot(tau, earlier, precision=lax.Precision.HIGHEST, preferred_element_type=f32)
            back = jnp.dot(tau, later, precision=lax.Precision.HIGHEST, preferred_element_type=f32)
            flip = jnp.broadcast_to(flips[pl.ds(b, 1), :].astype(f32), (LANES, LANES)).T
            before = jnp.where(flip != 0.0, back, front)
            common = jnp.exp(-before) * (1.0 - jnp.exp(-tau))
            for k in range(3):
                weight[k, x, at, :] = common * channel(v, coef[k])
            totals[pl.ds(b, 1), :] = compact(jnp.sum(tau, axis=1, keepdims=True))

        @pl.loop(1, nd)
        def _(j):
            total_copy(j).start()

    lead_way = (2 * l >= nl).astype(jnp.int32)
    n_lead = hops(lead_way)
    gap = jnp.where(2 * n_lead >= nl - 2, 5, NCH)
    prep_at = jnp.where(n_lead >= 4, 0, NCH)

    @pl.loop(0, 2 * NCH + 1)
    def _(item):
        @pl.when(item == prep_at)
        def _():
            prepare()

        @pl.when(item != prep_at)
        def _():
            k = item - (item > prep_at).astype(jnp.int32)
            both = NCH - gap
            e = k - gap
            mixed = (e >= 0) & (e < 2 * both)
            is_lead = (e < 0) | (mixed & (lax.rem(e + 2 * NCH, 2) == 0))
            half = lax.div(e + 2 * NCH, 2) - NCH
            i = jnp.where(e < 0, k, jnp.where(mixed, jnp.where(is_lead, gap + half, half), e - both))
            way = jnp.where(is_lead, lead_way, 1 - lead_way)
            step(way, i, is_lead)

    @pl.loop(1, nd)
    def _(j):
        peer = lax.rem(d + j, nd)
        wait_recv(gathered.at[peer], r_tot.at[peer])

    gathered[d] = totals[...]
    flip_px = flips[...] != 0
    offset = jnp.zeros((BLOCKS, LANES), f32)
    whole = jnp.zeros((BLOCKS, LANES), f32)
    for src in range(nd):
        got = gathered[src]
        whole = whole + got
        ahead = jnp.where(flip_px, src - d, d - src) > 0
        offset = offset + jnp.where(ahead, got, 0.0)
    through = jnp.exp(-offset)
    totals_scaled = 1.0 - jnp.exp(-whole)

    for b in range(BLOCKS):
        x = b // SL
        y = (b % SL) * LANES
        fwd = lev[0, x, 0, PAD + y + 4 * x : PAD + y + 4 * x + LANES, :]
        z = SL - 1 - x
        bwd = lev[1, z, 0, PAD + y + 4 * z : PAD + y + 4 * z + LANES, :]
        lit = AMBIENT + fwd + bwd
        for k in range(3):
            s = jnp.sum(weight[k, x, y : y + LANES, :] * lit, axis=1, keepdims=True)
            part[b, k : k + 1, :] = compact(s) * through[b : b + 1, :]
        part[b, 3:4, :] = totals_scaled[b : b + 1, :]

    def part_copy(j):
        peer = lax.rem(d + j, nd)
        return pltpu.make_async_remote_copy(
            src_ref=part.at[pl.ds(peer * mine, mine)],
            dst_ref=parts.at[d],
            send_sem=s_part.at[j],
            recv_sem=r_part.at[d],
            device_id=(l, peer),
            device_id_type=MESH,
        )

    @pl.loop(1, nd)
    def _(j):
        part_copy(j).start()

    own = part[pl.ds(d * mine, mine)]
    image = own

    @pl.loop(1, nd)
    def _(j):
        peer = lax.rem(d + j, nd)
        wait_recv(parts.at[peer], r_part.at[peer])

    parts[d] = own
    image = parts[0]
    for src in range(1, nd):
        image = image + parts[src]
    for m in range(mine):
        at = slice(m * LANES, (m + 1) * LANES)
        out[0:3, at] = image[m, 0:3, :]
        out[3:4, at] = own[m, 3:4, :]

    @pl.loop(1, nd)
    def _(j):
        total_copy(j).wait_send()
        part_copy(j).wait_send()

    for side, there in sides:

        @pl.when(there)
        def _():
            @pl.loop(0, NF)
            def _(i):
                fade_copy(side, i).wait_send()

    for way, first in ((0, 0), (1, nl - 1)):
        n = hops(way)
        odd = lax.rem(n, 2)

        @pl.loop(0, NCH)
        def _(i):
            for size, sent in sizes(n):

                @pl.when((n < nl - 1) & sent & (i >= odd))
                def _():
                    main_copy(way, i, size).wait_send()

            for side, there in sides:

                @pl.when(there & (n < nl - 1) & (lax.rem(n, 4) == 3) & (i >= odd))
                def _():
                    side_copy(way, side, i).wait_send()

                @pl.when(there & (l == first) & (i < NCH - 1))
                def _():
                    source_copy(way, side, i).wait_send()


def solution(mesh):
    nl, nd = mesh.shape["light"], mesh.shape["depth"]
    mine = BLOCKS // nd
    f32 = jnp.float32
    dma = pltpu.SemaphoreType.DMA

    def per_device(density, tf_table, tf_index, light_sources, spread_taps, view_flip):
        vmem = pl.BlockSpec(memory_space=pltpu.VMEM)
        smem = pl.BlockSpec(memory_space=pltpu.SMEM)
        return pl.pallas_call(
            functools.partial(kernel, nl, nd),
            out_shape=jax.ShapeDtypeStruct((4, mine * LANES), f32),
            in_specs=[vmem, smem, smem, vmem, smem, vmem],
            out_specs=vmem,
            scratch_shapes=[
                pltpu.VMEM((2, SL, 2, TALL, LANES), f32),
                pltpu.VMEM((2, NCH, 2 * CH, LANES), f32),
                pltpu.VMEM((2, NCH, 2 * CH, LANES), f32),
                pltpu.VMEM((2, 2, NCH, CH // 2, LANES), f32),
                pltpu.VMEM((2, 2, NCH, CH // 2, LANES), f32),
                pltpu.VMEM((SL, TALL, LANES), f32),
                pltpu.VMEM((2, SL, TALL, LANES), f32),
                pltpu.VMEM((2, 2, TALL, LANES), f32),
                pltpu.VMEM((3, SL, ROWS, LANES), f32),
                pltpu.VMEM((BLOCKS, LANES), f32),
                pltpu.VMEM((nd, BLOCKS, LANES), f32),
                pltpu.VMEM((BLOCKS, 8, LANES), f32),
                pltpu.VMEM((nd, mine, 8, LANES), f32),
                dma((2, NCH)),
                dma((2, NCH)),
                dma((2, 2, NCH)),
                dma((2, 2, NCH)),
                dma((2, NF)),
                dma((2, NF)),
                dma((nd,)),
                dma((nd,)),
                dma((nd,)),
                dma((nd,)),
            ],
            compiler_params=pltpu.CompilerParams(
                collective_id=0, has_side_effects=True, vmem_limit_bytes=48 << 20
            ),
            name="waves",
        )(density, tf_table, tf_index, light_sources, spread_taps, view_flip.reshape(BLOCKS, LANES))

    return jax.shard_map(
        per_device,
        mesh=mesh,
        in_specs=(
            P("light", None, "depth"),
            P(),
            P("light", "depth"),
            P(None, None, "depth"),
            P(),
            P("light"),
        ),
        out_specs=P(None, ("light", "depth")),
        check_vma=False,
    )
```

```python
import functools

import jax
import jax.numpy as jnp
from jax import lax
from jax.experimental import pallas as pl
from jax.experimental.pallas import tpu as pltpu
from jax.sharding import PartitionSpec as P

AMBIENT = 0.2
LIGHT_DEPTH = 36.0
VIEW_DEPTH = 16.0

SL = 4
ROWS = 512
LANES = 128
CH = 32
NCH = 17
PAD = 32
TALL = PAD + NCH * CH
FCH = 64
NF = ROWS // FCH
BLOCKS = SL * ROWS // LANES
MESH = pl.DeviceIdType.MESH


def channel(v, c):
    return jax.nn.sigmoid(((c[3] * v + c[2]) * v + c[1]) * v + c[0])


def kernel(
    nl,
    nd,
    dens_hbm,
    table,
    index,
    sources_hbm,
    taps,
    flips,
    out,
    dens,
    sources,
    lev,
    outbox,
    inbox,
    side_out,
    side_in,
    fade,
    fade_b,
    fade_out,
    fade_in,
    light_nb,
    weight,
    totals,
    gathered,
    part,
    parts,
    through,
    alpha,
    s_main,
    r_main,
    s_nb,
    r_nb,
    s_fade,
    r_fade,
    s_tot,
    r_tot,
    s_part,
    r_part,
    s_dens,
    s_src,
):
    l = lax.axis_index("light")
    d = lax.axis_index("depth")
    has_left = d > 0
    has_right = d < nd - 1
    f32 = jnp.float32

    barrier = pltpu.get_barrier_semaphore()

    def greet(to_l, to_d):
        pl.semaphore_signal(barrier, 1, device_id=(to_l, to_d), device_id_type=MESH)

    @pl.loop(1, nd)
    def _(j):
        greet(l, lax.rem(d + j, nd))

    for dl in (-1, 1):
        near = (l + dl >= 0) & (l + dl < nl)
        for dd in (-1, 0, 1):

            @pl.when(near & (d + dd >= 0) & (d + dd < nd))
            def _():
                greet(l + dl, d + dd)

    def dens_copy(i):
        rows = pl.ds(pl.multiple_of(i * FCH, FCH), FCH)
        return pltpu.make_async_copy(dens_hbm.at[:, rows, :], dens.at[:, rows, :], s_dens.at[i])

    def light_copy(way):
        return pltpu.make_async_copy(sources_hbm.at[way], sources.at[way], s_src.at[way])

    for way, first in ((0, 0), (1, nl - 1)):

        @pl.when(l == first)
        def _():
            light_copy(way).start()

    @pl.loop(0, NF)
    def _(i):
        dens_copy(i).start()

    zeros = jnp.zeros((PAD, LANES), f32)
    for way in range(2):
        for s in range(SL):
            for tile in range(2):
                lev[way, s, tile, 0:PAD, :] = zeros
        for tile in range(2):
            lev[way, 0, tile, PAD + ROWS : TALL, :] = zeros
    for x in range(SL):
        fade[x, 0:PAD, :] = zeros
        fade[x, PAD + ROWS : TALL, :] = zeros
        fade_b[x, 0:PAD, :] = zeros
        fade_b[x, PAD + ROWS : TALL, :] = zeros
    for side, there in ((0, has_left), (1, has_right)):

        @pl.when(jnp.logical_not(there))
        def _():
            @pl.loop(0, ROWS // CH)
            def _(i):
                at = pl.ds(pl.multiple_of(PAD + i * CH, CH), CH)
                for x in range(SL):
                    part_at = pl.ds(pl.multiple_of(16 * lax.rem(i, 2), 16), 16)
                    fade_in[side, lax.div(i, 2), x, part_at, :] = zeros[0:16]
                for way in range(2):
                    light_nb[way, side, at, :] = zeros
                    side_in[way, side, i, :, :] = zeros[0 : CH // 2]

    for way, first in ((0, 0), (1, nl - 1)):

        @pl.when(l == first)
        def _():
            light_copy(way).wait()

            @pl.loop(0, ROWS // CH)
            def _(i):
                lev[way, 0, 0, pl.ds(pl.multiple_of(PAD + i * CH, CH), CH), :] = sources[
                    way, pl.ds(pl.multiple_of(i * CH, CH), CH), :
                ]

    lane = lax.broadcasted_iota(jnp.int32, (CH, LANES), 1)
    low_half = lane < LANES // 2
    half_ch = CH // 2

    k_at = index[0, 0]
    coef = [[table[k_at, k, j] for j in range(4)] for k in range(4)]
    absorb = LIGHT_DEPTH / (SL * nl)
    thick = VIEW_DEPTH / (nd * LANES)

    beside = (has_left.astype(jnp.int32) + has_right.astype(jnp.int32)) + 1
    lights = (l > 0).astype(jnp.int32) + (l < nl - 1).astype(jnp.int32)
    pl.semaphore_wait(barrier, nd - 1 + lights * beside)

    def fade_copy(side, i):
        to = d - 1 + 2 * side
        return pltpu.make_async_remote_copy(
            src_ref=fade_out.at[side, i],
            dst_ref=fade_in.at[1 - side, i],
            send_sem=s_fade.at[side, i],
            recv_sem=r_fade.at[1 - side, i],
            device_id=(l, to),
            device_id_type=MESH,
        )

    def source_copy(way, side, j):
        return pltpu.make_async_remote_copy(
            src_ref=sources.at[way, pl.ds(pl.multiple_of(j * CH, CH), CH), :],
            dst_ref=light_nb.at[way, 1 - side, pl.ds(pl.multiple_of(PAD + j * CH, CH), CH), :],
            send_sem=s_nb.at[way, side, j],
            recv_sem=r_nb.at[way, 1 - side, j],
            device_id=(l, d - 1 + 2 * side),
            device_id_type=MESH,
        )

    sides = ((0, has_left), (1, has_right))

    @pl.loop(0, NF)
    def _(i):
        for side, there in sides:
            for way, first in ((0, 0), (1, nl - 1)):

                @pl.when(there & (l == first))
                def _():
                    source_copy(way, side, 2 * i).start()
                    source_copy(way, side, 2 * i + 1).start()

        src = pl.ds(pl.multiple_of(i * FCH, FCH), FCH)
        dst = pl.ds(pl.multiple_of(PAD + i * FCH, 32), FCH)
        dens_copy(i).wait()
        for x in range(SL):
            f = jnp.exp(-absorb * channel(dens[x, src, :], coef[3]))
            fade[x, dst, :] = f
            top, bottom = f[0:CH], f[CH:FCH]
            fade_out[0, i, x] = jnp.where(low_half, top, pltpu.roll(bottom, LANES // 2, 1))
            fade_out[1, i, x] = jnp.where(low_half, pltpu.roll(top, LANES // 2, 1), bottom)
        for side, there in sides:

            @pl.when(there)
            def _():
                fade_copy(side, i).start()

    total_tap = taps[0]
    for t in range(1, 9):
        total_tap = total_tap + taps[t]
    total_vec = jnp.full((8, LANES), total_tap, f32)
    tap = [(jnp.full((8, LANES), taps[t], f32) / total_vec)[0:1, :] for t in range(9)]

    def hops(way):
        return l + way * (nl - 1 - 2 * l)

    def sizes(n):
        m = lax.rem(n, 4)
        return ((CH, m == 3), (2 * CH, m == 0), (CH + CH // 2, (m == 1) | (m == 2)))

    def main_copy(way, i, size):
        return pltpu.make_async_remote_copy(
            src_ref=outbox.at[way, i, pl.ds(0, size), :],
            dst_ref=inbox.at[way, i - lax.rem(hops(way), 2), pl.ds(0, size), :],
            send_sem=s_main.at[way, i],
            recv_sem=r_main.at[way, i - lax.rem(hops(way), 2)],
            device_id=(l + 1 - 2 * way, d),
            device_id_type=MESH,
        )

    def side_copy(way, side, i):
        return pltpu.make_async_remote_copy(
            src_ref=side_out.at[way, side, i],
            dst_ref=side_in.at[way, 1 - side, i - 1],
            send_sem=s_nb.at[way, side, i],
            recv_sem=r_nb.at[way, 1 - side, i - 1],
            device_id=(l + 1 - 2 * way, d - 1 + 2 * side),
            device_id_type=MESH,
        )

    def wait_recv(dst, sem):
        pltpu.make_async_copy(dst, dst, sem).wait()

    def receive(way, i, lead):
        n = hops(way)
        odd = lax.rem(n, 2)
        base = pl.multiple_of(PAD + i * CH - 16 * odd, 16)
        rows = pl.ds(base, CH)

        early = (lax.rem(i, 2) == 0) & (i < 2 * NF)

        @pl.when(early & lead)
        def _():
            j = lax.div(i, 2)
            for side, there in sides:

                @pl.when(there)
                def _():
                    wait_recv(fade_in.at[side, j], r_fade.at[side, j])

            at = pl.multiple_of(PAD + i * CH, CH)
            for x in range(SL):
                lo = fade_in[0, j, x]
                hi = fade_in[1, j, x]
                fade_b[x, pl.ds(at, CH), :] = jnp.where(low_half, hi, pltpu.roll(lo, LANES // 2, 1))
                fade_b[x, pl.ds(at + CH, CH), :] = jnp.where(
                    low_half, pltpu.roll(hi, LANES // 2, 1), lo
                )

        for size, sent in sizes(n + 3):

            @pl.when((n > 0) & sent & (i < NCH - 1 + odd))
            def _():
                wait_recv(inbox.at[way, i, pl.ds(0, size), :], r_main.at[way, i])
                lev[way, 0, 0, rows, :] = inbox[way, i, 0:CH, :]
                if size == 2 * CH:
                    lev[way, 0, 1, rows, :] = inbox[way, i, CH : 2 * CH, :]
                elif size > CH:
                    near = inbox[way, i, CH:size, :]
                    lev[way, 0, 1, pl.ds(base, half_ch), :] = pltpu.roll(near, 96, 1)
                    lev[way, 0, 1, pl.ds(base + half_ch, half_ch), :] = pltpu.roll(near, 32, 1)

        @pl.when((lax.rem(n, 4) == 0) & (i < NCH - 1))
        def _():
            @pl.when(n == 0)
            def _():
                for side, there in sides:

                    @pl.when(there)
                    def _():
                        wait_recv(light_nb.at[way, side, rows, :], r_nb.at[way, side, i])

                lev[way, 0, 1, rows, :] = jnp.where(
                    low_half, light_nb[way, 1, rows, :], light_nb[way, 0, rows, :]
                )

            @pl.when(n > 0)
            def _():
                for side, there in sides:

                    @pl.when(there)
                    def _():
                        wait_recv(side_in.at[way, side, i], r_nb.at[way, side, i])

                lo = side_in[way, 0, i]
                hi = side_in[way, 1, i]
                low = low_half[0:half_ch]
                lev[way, 0, 1, pl.ds(base, half_ch), :] = jnp.where(
                    low, hi, pltpu.roll(lo, LANES // 2, 1)
                )
                lev[way, 0, 1, pl.ds(base + half_ch, half_ch), :] = jnp.where(
                    low, pltpu.roll(hi, LANES // 2, 1), lo
                )

    def slice_of(way, i, s):
        odd = lax.rem(hops(way), 2)
        base = pl.multiple_of(PAD + i * CH - 16 * odd, 16)
        layer = s + way * (SL - 1 - 2 * s)
        cols = []
        for tile in range(2):
            acc = tap[0] * lev[way, s, tile, pl.ds(base - 8, CH), :]
            for t in range(1, 9):
                acc = acc + tap[t] * lev[way, s, tile, pl.ds(base - 8 + t, CH), :]
            cols.append(acc)
        a, b = cols
        sum_a, sum_b = tap[4] * a, tap[4] * b
        for t in range(9):
            by = t - 4
            if by == 0:
                continue
            ra = pltpu.roll(a, (-by) % LANES, 1)
            rb = pltpu.roll(b, (-by) % LANES, 1)
            own = lane < LANES - by if by > 0 else lane >= -by
            sum_a = sum_a + tap[t] * jnp.where(own, ra, rb)
            sum_b = sum_b + tap[t] * jnp.where(own, rb, ra)
        there_rows = pl.ds(base - 4 * (s + 1), CH)
        fade_far = fade_b[layer, there_rows, :]
        return sum_a * fade[layer, there_rows, :], sum_b * fade_far

    def work(*chunks):
        for s in range(SL):
            got = [slice_of(way, i, s) for way, i in chunks]
            if s < SL - 1:
                for (way, i), (new_a, new_b) in zip(chunks, got):
                    odd = lax.rem(hops(way), 2)
                    rows = pl.ds(pl.multiple_of(PAD + i * CH - 16 * odd, 16), CH)
                    lev[way, s + 1, 0, rows, :] = new_a
                    lev[way, s + 1, 1, rows, :] = new_b
        for (way, i), (last_a, last_b) in zip(chunks, got):
            send(way, i, last_a, last_b)

    def send(way, i, last_a, last_b):
        n = hops(way)
        odd = lax.rem(n, 2)
        for size, sent in sizes(n):

            @pl.when((n < nl - 1) & sent & (i >= odd))
            def _():
                outbox[way, i, 0:CH, :] = last_a
                low = low_half[0:half_ch]
                if size == 2 * CH:
                    outbox[way, i, CH : 2 * CH, :] = last_b
                elif size > CH:
                    outbox[way, i, CH:size, :] = jnp.where(
                        low, pltpu.roll(last_b[0:half_ch], 32, 1), pltpu.roll(last_b[half_ch:CH], 96, 1)
                    )
                main_copy(way, i, size).start()
                if size == CH:
                    top, bottom = last_a[0:half_ch], last_a[half_ch:CH]
                    side_out[way, 0, i] = jnp.where(low, top, pltpu.roll(bottom, LANES // 2, 1))
                    side_out[way, 1, i] = jnp.where(low, pltpu.roll(top, LANES // 2, 1), bottom)
                    for side, there in sides:

                        @pl.when(there)
                        def _():
                            side_copy(way, side, i).start()

    row_i = lax.broadcasted_iota(jnp.int32, (LANES, LANES), 0)
    lane_i = lax.broadcasted_iota(jnp.int32, (LANES, LANES), 1)

    def compact(column):
        return jnp.sum(jnp.where(row_i == lane_i, column, 0.0), axis=0, keepdims=True)

    def total_copy(j):
        peer = lax.rem(d + j, nd)
        return pltpu.make_async_remote_copy(
            src_ref=totals,
            dst_ref=gathered.at[d],
            send_sem=s_tot.at[j],
            recv_sem=r_tot.at[d],
            device_id=(l, peer),
            device_id_type=MESH,
        )

    def prepare():
        earlier = (row_i < lane_i).astype(f32)
        later = (row_i > lane_i).astype(f32)

        @pl.loop(0, BLOCKS)
        def _(b):
            x = lax.div(b, SL)
            at = pl.ds(pl.multiple_of(lax.rem(b, SL) * LANES, LANES), LANES)
            v = dens[x, at, :]
            tau = thick * channel(v, coef[3])
            front = jnp.dot(tau, earlier, precision=lax.Precision.HIGHEST, preferred_element_type=f32)
            back = jnp.dot(tau, later, precision=lax.Precision.HIGHEST, preferred_element_type=f32)
            flip = jnp.broadcast_to(flips[pl.ds(b, 1), :].astype(f32), (LANES, LANES)).T
            before = jnp.where(flip != 0.0, back, front)
            common = jnp.exp(-before) * (1.0 - jnp.exp(-tau))
            for k in range(3):
                weight[k, x, at, :] = common * channel(v, coef[k])
            totals[pl.ds(b, 1), :] = compact(jnp.sum(tau, axis=1, keepdims=True))

        @pl.loop(1, nd)
        def _(j):
            total_copy(j).start()

    def offsets():
        @pl.loop(1, nd)
        def _(j):
            peer = lax.rem(d + j, nd)
            wait_recv(gathered.at[peer], r_tot.at[peer])

        gathered[d] = totals[...]
        flip_px = flips[...] != 0
        offset = jnp.zeros((BLOCKS, LANES), f32)
        whole = jnp.zeros((BLOCKS, LANES), f32)
        for src in range(nd):
            got = gathered[src]
            whole = whole + got
            ahead = jnp.where(flip_px, src - d, d - src) > 0
            offset = offset + jnp.where(ahead, got, 0.0)
        through[...] = jnp.exp(-offset)
        alpha[...] = 1.0 - jnp.exp(-whole)

    def part_copy(peer):
        return pltpu.make_async_remote_copy(
            src_ref=part.at[peer, 0:4],
            dst_ref=parts.at[d, 0:4],
            send_sem=s_part.at[peer],
            recv_sem=r_part.at[d],
            device_id=(l, peer),
            device_id_type=MESH,
        )

    def finish(g):
        y = pl.multiple_of(g * LANES, LANES)
        for x in range(SL):
            b = x * (ROWS // LANES) + g
            z = SL - 1 - x
            fwd = lev[0, x, 0, pl.ds(PAD + 4 * x + y, LANES), :]
            bwd = lev[1, z, 0, pl.ds(PAD + 4 * z + y, LANES), :]
            lit = AMBIENT + fwd + bwd
            for k in range(3):
                s = jnp.sum(weight[k, x, pl.ds(y, LANES), :] * lit, axis=1, keepdims=True)
                part[b, k : k + 1, :] = compact(s) * through[pl.ds(b, 1), :]

            @pl.when(b != d)
            def _():
                part_copy(b).start()

    lead_way = (2 * l >= nl).astype(jnp.int32)
    n_lead = hops(lead_way)
    gap = jnp.where(2 * n_lead >= nl - 2, 8, NCH)
    prep_at = jnp.where(n_lead >= 4, 0, NCH)

    @pl.loop(0, 2 * NCH + 1)
    def _(item):
        @pl.when(item == prep_at)
        def _():
            prepare()

        @pl.when(item != prep_at)
        def _():
            k = item - (item > prep_at).astype(jnp.int32)
            e = k - gap
            first_on = k < NCH
            second_on = (e >= 0) & (e < NCH)

            @pl.when(e == 0)
            def _():
                offsets()

            @pl.when(first_on & second_on)
            def _():
                receive(lead_way, k, True)
                receive(1 - lead_way, e, False)
                work((lead_way, k), (1 - lead_way, e))

            @pl.when(first_on != second_on)
            def _():
                i = jnp.where(first_on, k, e)
                way = jnp.where(first_on, lead_way, 1 - lead_way)
                receive(way, i, first_on)
                work((way, i))

            @pl.when(second_on & (e > 0) & (lax.rem(e, 4) == 0))
            def _():
                finish(lax.div(e, 4) - 1)

    @pl.loop(1, nd)
    def _(j):
        peer = lax.rem(d + j, nd)
        wait_recv(parts.at[peer, 0:4], r_part.at[peer])

    parts[d] = part[d]
    image = parts[0]
    for src in range(1, nd):
        image = image + parts[src]
    out[0:3, :] = image[0:3, :]
    out[3:4, :] = alpha[pl.ds(d, 1), :]

    @pl.loop(1, nd)
    def _(j):
        total_copy(j).wait_send()
        part_copy(lax.rem(d + j, nd)).wait_send()

    for side, there in sides:

        @pl.when(there)
        def _():
            @pl.loop(0, NF)
            def _(i):
                fade_copy(side, i).wait_send()

    for way, first in ((0, 0), (1, nl - 1)):
        n = hops(way)
        odd = lax.rem(n, 2)

        @pl.loop(0, NCH)
        def _(i):
            for size, sent in sizes(n):

                @pl.when((n < nl - 1) & sent & (i >= odd))
                def _():
                    main_copy(way, i, size).wait_send()

            for side, there in sides:

                @pl.when(there & (n < nl - 1) & (lax.rem(n, 4) == 3) & (i >= odd))
                def _():
                    side_copy(way, side, i).wait_send()

                @pl.when(there & (l == first) & (i < NCH - 1))
                def _():
                    source_copy(way, side, i).wait_send()


def solution(mesh):
    nl, nd = mesh.shape["light"], mesh.shape["depth"]
    mine = BLOCKS // nd
    f32 = jnp.float32
    dma = pltpu.SemaphoreType.DMA

    def per_device(density, tf_table, tf_index, light_sources, spread_taps, view_flip):
        vmem = pl.BlockSpec(memory_space=pltpu.VMEM)
        anywhere = pl.BlockSpec(memory_space=pl.ANY)
        smem = pl.BlockSpec(memory_space=pltpu.SMEM)
        return pl.pallas_call(
            functools.partial(kernel, nl, nd),
            out_shape=jax.ShapeDtypeStruct((4, mine * LANES), f32),
            in_specs=[anywhere, smem, smem, anywhere, smem, vmem],
            out_specs=vmem,
            scratch_shapes=[
                pltpu.VMEM((SL, ROWS, LANES), f32),
                pltpu.VMEM((2, ROWS, LANES), f32),
                pltpu.VMEM((2, SL, 2, TALL, LANES), f32),
                pltpu.VMEM((2, NCH, 2 * CH, LANES), f32),
                pltpu.VMEM((2, NCH, 2 * CH, LANES), f32),
                pltpu.VMEM((2, 2, NCH, CH // 2, LANES), f32),
                pltpu.VMEM((2, 2, NCH, CH // 2, LANES), f32),
                pltpu.VMEM((SL, TALL, LANES), f32),
                pltpu.VMEM((SL, TALL, LANES), f32),
                pltpu.VMEM((2, NF, SL, CH, LANES), f32),
                pltpu.VMEM((2, NF, SL, CH, LANES), f32),
                pltpu.VMEM((2, 2, TALL, LANES), f32),
                pltpu.VMEM((3, SL, ROWS, LANES), f32),
                pltpu.VMEM((BLOCKS, LANES), f32),
                pltpu.VMEM((nd, BLOCKS, LANES), f32),
                pltpu.VMEM((BLOCKS, 8, LANES), f32),
                pltpu.VMEM((nd, 8, LANES), f32),
                pltpu.VMEM((BLOCKS, LANES), f32),
                pltpu.VMEM((BLOCKS, LANES), f32),
                dma((2, NCH)),
                dma((2, NCH)),
                dma((2, 2, NCH)),
                dma((2, 2, NCH)),
                dma((2, NF)),
                dma((2, NF)),
                dma((nd,)),
                dma((nd,)),
                dma((nd,)),
                dma((nd,)),
                dma((NF,)),
                dma((2,)),
            ],
            compiler_params=pltpu.CompilerParams(
                collective_id=0, has_side_effects=True, vmem_limit_bytes=48 << 20
            ),
            name="waves",
        )(density, tf_table, tf_index, light_sources, spread_taps, view_flip.reshape(BLOCKS, LANES))

    return jax.shard_map(
        per_device,
        mesh=mesh,
        in_specs=(
            P("light", None, "depth"),
            P(),
            P("light", "depth"),
            P(None, None, "depth"),
            P(),
            P("light"),
        ),
        out_specs=P(None, ("light", "depth")),
        check_vma=False,
    )
```

```python
import functools

import jax
import jax.numpy as jnp
from jax import lax
from jax.experimental import pallas as pl
from jax.experimental.pallas import tpu as pltpu
from jax.sharding import PartitionSpec as P

AMBIENT = 0.2
LIGHT_DEPTH = 36.0
VIEW_DEPTH = 16.0

SL = 4
ROWS = 512
LANES = 128
CH = 32
NCH = 17
PAD = 32
TALL = PAD + NCH * CH
FCH = 64
NF = ROWS // FCH
BLOCKS = SL * ROWS // LANES
MESH = pl.DeviceIdType.MESH


def channel(v, c):
    return jax.nn.sigmoid(((c[3] * v + c[2]) * v + c[1]) * v + c[0])


def kernel(
    nl,
    nd,
    dens_hbm,
    table,
    index,
    sources_hbm,
    taps,
    flips,
    out,
    dens,
    sources,
    lev,
    outbox,
    inbox,
    side_out,
    side_in,
    fade,
    fade_b,
    fade_out,
    fade_in,
    light_nb,
    weight,
    totals,
    gathered,
    part,
    parts,
    through,
    alpha,
    s_main,
    r_main,
    s_nb,
    r_nb,
    s_fade,
    r_fade,
    s_tot,
    r_tot,
    s_part,
    r_part,
    s_dens,
    s_src,
):
    l = lax.axis_index("light")
    d = lax.axis_index("depth")
    has_left = d > 0
    has_right = d < nd - 1
    f32 = jnp.float32

    barrier = pltpu.get_barrier_semaphore()

    def greet(to_l, to_d):
        pl.semaphore_signal(barrier, 1, device_id=(to_l, to_d), device_id_type=MESH)

    @pl.loop(1, nd)
    def _(j):
        greet(l, lax.rem(d + j, nd))

    for dl in (-1, 1):
        near = (l + dl >= 0) & (l + dl < nl)
        for dd in (-1, 0, 1):

            @pl.when(near & (d + dd >= 0) & (d + dd < nd))
            def _():
                greet(l + dl, d + dd)

    def dens_copy(i):
        rows = pl.ds(pl.multiple_of(i * FCH, FCH), FCH)
        return pltpu.make_async_copy(dens_hbm.at[:, rows, :], dens.at[:, rows, :], s_dens.at[i])

    def light_copy(way):
        return pltpu.make_async_copy(sources_hbm.at[way], sources.at[way], s_src.at[way])

    for way, first in ((0, 0), (1, nl - 1)):

        @pl.when(l == first)
        def _():
            light_copy(way).start()

    @pl.loop(0, NF)
    def _(i):
        dens_copy(i).start()

    zeros = jnp.zeros((PAD, LANES), f32)
    for way in range(2):
        for s in range(SL):
            for tile in range(2):
                lev[way, s, tile, 0:PAD, :] = zeros
        for tile in range(2):
            lev[way, 0, tile, PAD + ROWS : TALL, :] = zeros
    for x in range(SL):
        fade[x, 0:PAD, :] = zeros
        fade[x, PAD + ROWS : TALL, :] = zeros
        fade_b[x, 0:PAD, :] = zeros
        fade_b[x, PAD + ROWS : TALL, :] = zeros
    for side, there in ((0, has_left), (1, has_right)):

        @pl.when(jnp.logical_not(there))
        def _():
            @pl.loop(0, ROWS // CH)
            def _(i):
                at = pl.ds(pl.multiple_of(PAD + i * CH, CH), CH)
                for x in range(SL):
                    part_at = pl.ds(pl.multiple_of(16 * lax.rem(i, 2), 16), 16)
                    fade_in[side, lax.div(i, 2), x, part_at, :] = zeros[0:16]
                for way in range(2):
                    light_nb[way, side, at, :] = zeros
                    side_in[way, side, i, :, :] = zeros[0 : CH // 2]

    for way, first in ((0, 0), (1, nl - 1)):

        @pl.when(l == first)
        def _():
            light_copy(way).wait()

            @pl.loop(0, ROWS // CH)
            def _(i):
                lev[way, 0, 0, pl.ds(pl.multiple_of(PAD + i * CH, CH), CH), :] = sources[
                    way, pl.ds(pl.multiple_of(i * CH, CH), CH), :
                ]

    lane = lax.broadcasted_iota(jnp.int32, (CH, LANES), 1)
    low_half = lane < LANES // 2
    half_ch = CH // 2

    k_at = index[0, 0]
    coef = [[table[k_at, k, j] for j in range(4)] for k in range(4)]
    absorb = LIGHT_DEPTH / (SL * nl)
    thick = VIEW_DEPTH / (nd * LANES)

    beside = (has_left.astype(jnp.int32) + has_right.astype(jnp.int32)) + 1
    lights = (l > 0).astype(jnp.int32) + (l < nl - 1).astype(jnp.int32)
    pl.semaphore_wait(barrier, nd - 1 + lights * beside)

    def fade_copy(side, i):
        to = d - 1 + 2 * side
        return pltpu.make_async_remote_copy(
            src_ref=fade_out.at[side, i],
            dst_ref=fade_in.at[1 - side, i],
            send_sem=s_fade.at[side, i],
            recv_sem=r_fade.at[1 - side, i],
            device_id=(l, to),
            device_id_type=MESH,
        )

    def source_copy(way, side, j):
        return pltpu.make_async_remote_copy(
            src_ref=sources.at[way, pl.ds(pl.multiple_of(j * CH, CH), CH), :],
            dst_ref=light_nb.at[way, 1 - side, pl.ds(pl.multiple_of(PAD + j * CH, CH), CH), :],
            send_sem=s_nb.at[way, side, j],
            recv_sem=r_nb.at[way, 1 - side, j],
            device_id=(l, d - 1 + 2 * side),
            device_id_type=MESH,
        )

    sides = ((0, has_left), (1, has_right))

    @pl.loop(0, NF)
    def _(i):
        for side, there in sides:
            for way, first in ((0, 0), (1, nl - 1)):

                @pl.when(there & (l == first))
                def _():
                    source_copy(way, side, 2 * i).start()
                    source_copy(way, side, 2 * i + 1).start()

        src = pl.ds(pl.multiple_of(i * FCH, FCH), FCH)
        dst = pl.ds(pl.multiple_of(PAD + i * FCH, 32), FCH)
        dens_copy(i).wait()
        for x in range(SL):
            f = jnp.exp(-absorb * channel(dens[x, src, :], coef[3]))
            fade[x, dst, :] = f
            top, bottom = f[0:CH], f[CH:FCH]
            fade_out[0, i, x] = jnp.where(low_half, top, pltpu.roll(bottom, LANES // 2, 1))
            fade_out[1, i, x] = jnp.where(low_half, pltpu.roll(top, LANES // 2, 1), bottom)
        for side, there in sides:

            @pl.when(there)
            def _():
                fade_copy(side, i).start()

    total_tap = taps[0]
    for t in range(1, 9):
        total_tap = total_tap + taps[t]
    total_vec = jnp.full((8, LANES), total_tap, f32)
    tap = [(jnp.full((8, LANES), taps[t], f32) / total_vec)[0:1, :] for t in range(9)]

    def hops(way):
        return l + way * (nl - 1 - 2 * l)

    def sizes(n):
        m = lax.rem(n, 4)
        return ((CH, m == 3), (2 * CH, m == 0), (CH + CH // 2, (m == 1) | (m == 2)))

    def main_copy(way, i, size):
        return pltpu.make_async_remote_copy(
            src_ref=outbox.at[way, i, pl.ds(0, size), :],
            dst_ref=inbox.at[way, i - lax.rem(hops(way), 2), pl.ds(0, size), :],
            send_sem=s_main.at[way, i],
            recv_sem=r_main.at[way, i - lax.rem(hops(way), 2)],
            device_id=(l + 1 - 2 * way, d),
            device_id_type=MESH,
        )

    def side_copy(way, side, i):
        return pltpu.make_async_remote_copy(
            src_ref=side_out.at[way, side, i],
            dst_ref=side_in.at[way, 1 - side, i - 1],
            send_sem=s_nb.at[way, side, i],
            recv_sem=r_nb.at[way, 1 - side, i - 1],
            device_id=(l + 1 - 2 * way, d - 1 + 2 * side),
            device_id_type=MESH,
        )

    def wait_recv(dst, sem):
        pltpu.make_async_copy(dst, dst, sem).wait()

    def receive(way, i, lead):
        n = hops(way)
        odd = lax.rem(n, 2)
        base = pl.multiple_of(PAD + i * CH - 16 * odd, 16)
        rows = pl.ds(base, CH)

        early = (lax.rem(i, 2) == 0) & (i < 2 * NF)

        @pl.when(early & lead)
        def _():
            j = lax.div(i, 2)
            for side, there in sides:

                @pl.when(there)
                def _():
                    wait_recv(fade_in.at[side, j], r_fade.at[side, j])

            at = pl.multiple_of(PAD + i * CH, CH)
            for x in range(SL):
                lo = fade_in[0, j, x]
                hi = fade_in[1, j, x]
                fade_b[x, pl.ds(at, CH), :] = jnp.where(low_half, hi, pltpu.roll(lo, LANES // 2, 1))
                fade_b[x, pl.ds(at + CH, CH), :] = jnp.where(
                    low_half, pltpu.roll(hi, LANES // 2, 1), lo
                )

        for size, sent in sizes(n + 3):

            @pl.when((n > 0) & sent & (i < NCH - 1 + odd))
            def _():
                wait_recv(inbox.at[way, i, pl.ds(0, size), :], r_main.at[way, i])
                lev[way, 0, 0, rows, :] = inbox[way, i, 0:CH, :]
                if size == 2 * CH:
                    lev[way, 0, 1, rows, :] = inbox[way, i, CH : 2 * CH, :]
                elif size > CH:
                    near = inbox[way, i, CH:size, :]
                    lev[way, 0, 1, pl.ds(base, half_ch), :] = pltpu.roll(near, 96, 1)
                    lev[way, 0, 1, pl.ds(base + half_ch, half_ch), :] = pltpu.roll(near, 32, 1)

        @pl.when((lax.rem(n, 4) == 0) & (i < NCH - 1))
        def _():
            @pl.when(n == 0)
            def _():
                for side, there in sides:

                    @pl.when(there)
                    def _():
                        wait_recv(light_nb.at[way, side, rows, :], r_nb.at[way, side, i])

                lev[way, 0, 1, rows, :] = jnp.where(
                    low_half, light_nb[way, 1, rows, :], light_nb[way, 0, rows, :]
                )

            @pl.when(n > 0)
            def _():
                for side, there in sides:

                    @pl.when(there)
                    def _():
                        wait_recv(side_in.at[way, side, i], r_nb.at[way, side, i])

                lo = side_in[way, 0, i]
                hi = side_in[way, 1, i]
                low = low_half[0:half_ch]
                lev[way, 0, 1, pl.ds(base, half_ch), :] = jnp.where(
                    low, hi, pltpu.roll(lo, LANES // 2, 1)
                )
                lev[way, 0, 1, pl.ds(base + half_ch, half_ch), :] = jnp.where(
                    low, pltpu.roll(hi, LANES // 2, 1), lo
                )

    def added(terms):
        while len(terms) > 1:
            terms = [sum(terms[j + 1 : j + 2], terms[j]) for j in range(0, len(terms), 2)]
        return terms[0]

    def slice_of(way, i, s):
        odd = lax.rem(hops(way), 2)
        base = pl.multiple_of(PAD + i * CH - 16 * odd, 16)
        layer = s + way * (SL - 1 - 2 * s)
        cols = []
        for tile in range(2):
            cols.append(
                added([tap[t] * lev[way, s, tile, pl.ds(base - 8 + t, CH), :] for t in range(9)])
            )
        a, b = cols
        sum_a, sum_b = tap[4] * a, tap[4] * b
        for t in range(9):
            by = t - 4
            if by == 0:
                continue
            ra = pltpu.roll(a, (-by) % LANES, 1)
            rb = pltpu.roll(b, (-by) % LANES, 1)
            own = lane < LANES - by if by > 0 else lane >= -by
            sum_a = sum_a + tap[t] * jnp.where(own, ra, rb)
            sum_b = sum_b + tap[t] * jnp.where(own, rb, ra)
        there_rows = pl.ds(base - 4 * (s + 1), CH)
        fade_far = fade_b[layer, there_rows, :]
        return sum_a * fade[layer, there_rows, :], sum_b * fade_far

    def work(*chunks):
        for s in range(SL):
            got = [slice_of(way, i, s) for way, i in chunks]
            if s < SL - 1:
                for (way, i), (new_a, new_b) in zip(chunks, got):
                    odd = lax.rem(hops(way), 2)
                    rows = pl.ds(pl.multiple_of(PAD + i * CH - 16 * odd, 16), CH)
                    lev[way, s + 1, 0, rows, :] = new_a
                    lev[way, s + 1, 1, rows, :] = new_b
        for (way, i), (last_a, last_b) in zip(chunks, got):
            send(way, i, last_a, last_b)

    def send(way, i, last_a, last_b):
        n = hops(way)
        odd = lax.rem(n, 2)
        for size, sent in sizes(n):

            @pl.when((n < nl - 1) & sent & (i >= odd))
            def _():
                outbox[way, i, 0:CH, :] = last_a
                low = low_half[0:half_ch]
                if size == 2 * CH:
                    outbox[way, i, CH : 2 * CH, :] = last_b
                elif size > CH:
                    outbox[way, i, CH:size, :] = jnp.where(
                        low, pltpu.roll(last_b[0:half_ch], 32, 1), pltpu.roll(last_b[half_ch:CH], 96, 1)
                    )
                main_copy(way, i, size).start()
                if size == CH:
                    top, bottom = last_a[0:half_ch], last_a[half_ch:CH]
                    side_out[way, 0, i] = jnp.where(low, top, pltpu.roll(bottom, LANES // 2, 1))
                    side_out[way, 1, i] = jnp.where(low, pltpu.roll(top, LANES // 2, 1), bottom)
                    for side, there in sides:

                        @pl.when(there)
                        def _():
                            side_copy(way, side, i).start()

    row_i = lax.broadcasted_iota(jnp.int32, (LANES, LANES), 0)
    lane_i = lax.broadcasted_iota(jnp.int32, (LANES, LANES), 1)

    def compact(column):
        return jnp.sum(jnp.where(row_i == lane_i, column, 0.0), axis=0, keepdims=True)

    def total_copy(j):
        peer = lax.rem(d + j, nd)
        return pltpu.make_async_remote_copy(
            src_ref=totals,
            dst_ref=gathered.at[d],
            send_sem=s_tot.at[j],
            recv_sem=r_tot.at[d],
            device_id=(l, peer),
            device_id_type=MESH,
        )

    def prepare():
        earlier = (row_i < lane_i).astype(f32)
        later = (row_i > lane_i).astype(f32)

        @pl.loop(0, BLOCKS)
        def _(b):
            x = lax.div(b, SL)
            at = pl.ds(pl.multiple_of(lax.rem(b, SL) * LANES, LANES), LANES)
            v = dens[x, at, :]
            tau = thick * channel(v, coef[3])
            front = jnp.dot(tau, earlier, precision=lax.Precision.HIGHEST, preferred_element_type=f32)
            back = jnp.dot(tau, later, precision=lax.Precision.HIGHEST, preferred_element_type=f32)
            flip = jnp.broadcast_to(flips[pl.ds(b, 1), :].astype(f32), (LANES, LANES)).T
            before = jnp.where(flip != 0.0, back, front)
            common = jnp.exp(-before) * (1.0 - jnp.exp(-tau))
            for k in range(3):
                weight[k, x, at, :] = common * channel(v, coef[k])
            totals[pl.ds(b, 1), :] = compact(jnp.sum(tau, axis=1, keepdims=True))

        @pl.loop(1, nd)
        def _(j):
            total_copy(j).start()

    def offsets():
        @pl.loop(1, nd)
        def _(j):
            peer = lax.rem(d + j, nd)
            wait_recv(gathered.at[peer], r_tot.at[peer])

        gathered[d] = totals[...]
        flip_px = flips[...] != 0
        offset = jnp.zeros((BLOCKS, LANES), f32)
        whole = jnp.zeros((BLOCKS, LANES), f32)
        for src in range(nd):
            got = gathered[src]
            whole = whole + got
            ahead = jnp.where(flip_px, src - d, d - src) > 0
            offset = offset + jnp.where(ahead, got, 0.0)
        through[...] = jnp.exp(-offset)
        alpha[...] = 1.0 - jnp.exp(-whole)

    def part_copy(peer):
        return pltpu.make_async_remote_copy(
            src_ref=part.at[peer, 0:4],
            dst_ref=parts.at[d, 0:4],
            send_sem=s_part.at[peer],
            recv_sem=r_part.at[d],
            device_id=(l, peer),
            device_id_type=MESH,
        )

    def finish(g):
        y = pl.multiple_of(g * LANES, LANES)
        for x in range(SL):
            b = x * (ROWS // LANES) + g
            z = SL - 1 - x
            fwd = lev[0, x, 0, pl.ds(PAD + 4 * x + y, LANES), :]
            bwd = lev[1, z, 0, pl.ds(PAD + 4 * z + y, LANES), :]
            lit = AMBIENT + fwd + bwd
            for k in range(3):
                s = jnp.sum(weight[k, x, pl.ds(y, LANES), :] * lit, axis=1, keepdims=True)
                part[b, k : k + 1, :] = compact(s) * through[pl.ds(b, 1), :]

            @pl.when(b != d)
            def _():
                part_copy(b).start()

    lead_way = (2 * l >= nl).astype(jnp.int32)
    n_lead = hops(lead_way)
    gap = jnp.where(2 * n_lead >= nl - 2, 8, NCH)
    prep_at = jnp.where(n_lead >= 4, 0, NCH)

    @pl.loop(0, 2 * NCH + 1)
    def _(item):
        @pl.when(item == prep_at)
        def _():
            prepare()

        @pl.when(item != prep_at)
        def _():
            k = item - (item > prep_at).astype(jnp.int32)
            e = k - gap
            first_on = k < NCH
            second_on = (e >= 0) & (e < NCH)

            @pl.when(e == 0)
            def _():
                offsets()

            @pl.when(first_on & second_on)
            def _():
                receive(lead_way, k, True)
                receive(1 - lead_way, e, False)
                work((lead_way, k), (1 - lead_way, e))

            @pl.when(first_on != second_on)
            def _():
                i = jnp.where(first_on, k, e)
                way = jnp.where(first_on, lead_way, 1 - lead_way)
                receive(way, i, first_on)
                work((way, i))

            @pl.when(second_on & (e > 0) & (lax.rem(e, 4) == 0))
            def _():
                finish(lax.div(e, 4) - 1)

    @pl.loop(1, nd)
    def _(j):
        peer = lax.rem(d + j, nd)
        wait_recv(parts.at[peer, 0:4], r_part.at[peer])

    parts[d] = part[d]
    image = parts[0]
    for src in range(1, nd):
        image = image + parts[src]
    out[0:3, :] = image[0:3, :]
    out[3:4, :] = alpha[pl.ds(d, 1), :]

    @pl.loop(1, nd)
    def _(j):
        total_copy(j).wait_send()
        part_copy(lax.rem(d + j, nd)).wait_send()

    for side, there in sides:

        @pl.when(there)
        def _():
            @pl.loop(0, NF)
            def _(i):
                fade_copy(side, i).wait_send()

    for way, first in ((0, 0), (1, nl - 1)):
        n = hops(way)
        odd = lax.rem(n, 2)

        @pl.loop(0, NCH)
        def _(i):
            for size, sent in sizes(n):

                @pl.when((n < nl - 1) & sent & (i >= odd))
                def _():
                    main_copy(way, i, size).wait_send()

            for side, there in sides:

                @pl.when(there & (n < nl - 1) & (lax.rem(n, 4) == 3) & (i >= odd))
                def _():
                    side_copy(way, side, i).wait_send()

                @pl.when(there & (l == first) & (i < NCH - 1))
                def _():
                    source_copy(way, side, i).wait_send()


def solution(mesh):
    nl, nd = mesh.shape["light"], mesh.shape["depth"]
    mine = BLOCKS // nd
    f32 = jnp.float32
    dma = pltpu.SemaphoreType.DMA

    def per_device(density, tf_table, tf_index, light_sources, spread_taps, view_flip):
        vmem = pl.BlockSpec(memory_space=pltpu.VMEM)
        anywhere = pl.BlockSpec(memory_space=pl.ANY)
        smem = pl.BlockSpec(memory_space=pltpu.SMEM)
        return pl.pallas_call(
            functools.partial(kernel, nl, nd),
            out_shape=jax.ShapeDtypeStruct((4, mine * LANES), f32),
            in_specs=[anywhere, smem, smem, anywhere, smem, vmem],
            out_specs=vmem,
            scratch_shapes=[
                pltpu.VMEM((SL, ROWS, LANES), f32),
                pltpu.VMEM((2, ROWS, LANES), f32),
                pltpu.VMEM((2, SL, 2, TALL, LANES), f32),
                pltpu.VMEM((2, NCH, 2 * CH, LANES), f32),
                pltpu.VMEM((2, NCH, 2 * CH, LANES), f32),
                pltpu.VMEM((2, 2, NCH, CH // 2, LANES), f32),
                pltpu.VMEM((2, 2, NCH, CH // 2, LANES), f32),
                pltpu.VMEM((SL, TALL, LANES), f32),
                pltpu.VMEM((SL, TALL, LANES), f32),
                pltpu.VMEM((2, NF, SL, CH, LANES), f32),
                pltpu.VMEM((2, NF, SL, CH, LANES), f32),
                pltpu.VMEM((2, 2, TALL, LANES), f32),
                pltpu.VMEM((3, SL, ROWS, LANES), f32),
                pltpu.VMEM((BLOCKS, LANES), f32),
                pltpu.VMEM((nd, BLOCKS, LANES), f32),
                pltpu.VMEM((BLOCKS, 8, LANES), f32),
                pltpu.VMEM((nd, 8, LANES), f32),
                pltpu.VMEM((BLOCKS, LANES), f32),
                pltpu.VMEM((BLOCKS, LANES), f32),
                dma((2, NCH)),
                dma((2, NCH)),
                dma((2, 2, NCH)),
                dma((2, 2, NCH)),
                dma((2, NF)),
                dma((2, NF)),
                dma((nd,)),
                dma((nd,)),
                dma((nd,)),
                dma((nd,)),
                dma((NF,)),
                dma((2,)),
            ],
            compiler_params=pltpu.CompilerParams(
                collective_id=0, has_side_effects=True, vmem_limit_bytes=48 << 20
            ),
            name="waves",
        )(density, tf_table, tf_index, light_sources, spread_taps, view_flip.reshape(BLOCKS, LANES))

    return jax.shard_map(
        per_device,
        mesh=mesh,
        in_specs=(
            P("light", None, "depth"),
            P(),
            P("light", "depth"),
            P(None, None, "depth"),
            P(),
            P("light"),
        ),
        out_specs=P(None, ("light", "depth")),
        check_vma=False,
    )
```

```python
import functools

import jax
import jax.numpy as jnp
from jax import lax
from jax.experimental import pallas as pl
from jax.experimental.pallas import tpu as pltpu
from jax.sharding import PartitionSpec as P

AMBIENT = 0.2
LIGHT_DEPTH = 36.0
VIEW_DEPTH = 16.0

SL = 4
ROWS = 512
LANES = 128
CH = 32
NCH = 17
PAD = 32
TALL = PAD + NCH * CH
FCH = 64
NF = ROWS // FCH
BLOCKS = SL * ROWS // LANES
MESH = pl.DeviceIdType.MESH


def channel(v, c):
    return jax.nn.sigmoid(((c[3] * v + c[2]) * v + c[1]) * v + c[0])


def kernel(
    nl,
    nd,
    dens_hbm,
    table,
    index,
    sources_hbm,
    taps,
    flips,
    out,
    dens,
    sources,
    lev,
    outbox,
    inbox,
    side_out,
    side_in,
    fade,
    fade_b,
    fade_out,
    fade_in,
    light_nb,
    weight,
    totals,
    gathered,
    part,
    parts,
    through,
    alpha,
    s_main,
    r_main,
    s_nb,
    r_nb,
    s_fade,
    r_fade,
    s_tot,
    r_tot,
    s_part,
    r_part,
    s_dens,
    s_src,
):
    l = lax.axis_index("light")
    d = lax.axis_index("depth")
    has_left = d > 0
    has_right = d < nd - 1
    f32 = jnp.float32

    barrier = pltpu.get_barrier_semaphore()

    def greet(to_l, to_d):
        pl.semaphore_signal(barrier, 1, device_id=(to_l, to_d), device_id_type=MESH)

    @pl.loop(1, nd)
    def _(j):
        greet(l, lax.rem(d + j, nd))

    for dl in (-1, 1):
        near = (l + dl >= 0) & (l + dl < nl)
        for dd in (-1, 0, 1):

            @pl.when(near & (d + dd >= 0) & (d + dd < nd))
            def _():
                greet(l + dl, d + dd)

    def dens_copy(i):
        rows = pl.ds(pl.multiple_of(i * FCH, FCH), FCH)
        return pltpu.make_async_copy(dens_hbm.at[:, rows, :], dens.at[:, rows, :], s_dens.at[i])

    def light_copy(way):
        return pltpu.make_async_copy(sources_hbm.at[way], sources.at[way], s_src.at[way])

    for way, first in ((0, 0), (1, nl - 1)):

        @pl.when(l == first)
        def _():
            light_copy(way).start()

    @pl.loop(0, NF)
    def _(i):
        dens_copy(i).start()

    zeros = jnp.zeros((PAD, LANES), f32)
    for way in range(2):
        for s in range(SL):
            for tile in range(2):
                lev[way, s, tile, 0:PAD, :] = zeros
        for tile in range(2):
            lev[way, 0, tile, PAD + ROWS : TALL, :] = zeros
    for x in range(SL):
        fade[x, 0:PAD, :] = zeros
        fade[x, PAD + ROWS : TALL, :] = zeros
        fade_b[x, 0:PAD, :] = zeros
        fade_b[x, PAD + ROWS : TALL, :] = zeros
    for side, there in ((0, has_left), (1, has_right)):

        @pl.when(jnp.logical_not(there))
        def _():
            @pl.loop(0, ROWS // CH)
            def _(i):
                at = pl.ds(pl.multiple_of(PAD + i * CH, CH), CH)
                for x in range(SL):
                    part_at = pl.ds(pl.multiple_of(16 * lax.rem(i, 2), 16), 16)
                    fade_in[side, lax.div(i, 2), x, part_at, :] = zeros[0:16]
                for way in range(2):
                    light_nb[way, side, at, :] = zeros
                    side_in[way, side, i, :, :] = zeros[0 : CH // 2]

    for way, first in ((0, 0), (1, nl - 1)):

        @pl.when(l == first)
        def _():
            light_copy(way).wait()

            @pl.loop(0, ROWS // CH)
            def _(i):
                lev[way, 0, 0, pl.ds(pl.multiple_of(PAD + i * CH, CH), CH), :] = sources[
                    way, pl.ds(pl.multiple_of(i * CH, CH), CH), :
                ]

    lane = lax.broadcasted_iota(jnp.int32, (CH, LANES), 1)
    low_half = lane < LANES // 2
    half_ch = CH // 2

    k_at = index[0, 0]
    coef = [[table[k_at, k, j] for j in range(4)] for k in range(4)]
    absorb = LIGHT_DEPTH / (SL * nl)
    thick = VIEW_DEPTH / (nd * LANES)

    beside = (has_left.astype(jnp.int32) + has_right.astype(jnp.int32)) + 1
    lights = (l > 0).astype(jnp.int32) + (l < nl - 1).astype(jnp.int32)
    pl.semaphore_wait(barrier, nd - 1 + lights * beside)

    def fade_copy(side, i):
        to = d - 1 + 2 * side
        return pltpu.make_async_remote_copy(
            src_ref=fade_out.at[side, i],
            dst_ref=fade_in.at[1 - side, i],
            send_sem=s_fade.at[side, i],
            recv_sem=r_fade.at[1 - side, i],
            device_id=(l, to),
            device_id_type=MESH,
        )

    def source_copy(way, side, j):
        return pltpu.make_async_remote_copy(
            src_ref=sources.at[way, pl.ds(pl.multiple_of(j * CH, CH), CH), :],
            dst_ref=light_nb.at[way, 1 - side, pl.ds(pl.multiple_of(PAD + j * CH, CH), CH), :],
            send_sem=s_nb.at[way, side, j],
            recv_sem=r_nb.at[way, 1 - side, j],
            device_id=(l, d - 1 + 2 * side),
            device_id_type=MESH,
        )

    sides = ((0, has_left), (1, has_right))

    @pl.loop(0, NF)
    def _(i):
        for side, there in sides:
            for way, first in ((0, 0), (1, nl - 1)):

                @pl.when(there & (l == first))
                def _():
                    source_copy(way, side, 2 * i).start()
                    source_copy(way, side, 2 * i + 1).start()

        src = pl.ds(pl.multiple_of(i * FCH, FCH), FCH)
        dst = pl.ds(pl.multiple_of(PAD + i * FCH, 32), FCH)
        dens_copy(i).wait()
        for x in range(SL):
            f = jnp.exp(-absorb * channel(dens[x, src, :], coef[3]))
            fade[x, dst, :] = f
            top, bottom = f[0:CH], f[CH:FCH]
            fade_out[0, i, x] = jnp.where(low_half, top, pltpu.roll(bottom, LANES // 2, 1))
            fade_out[1, i, x] = jnp.where(low_half, pltpu.roll(top, LANES // 2, 1), bottom)
        for side, there in sides:

            @pl.when(there)
            def _():
                fade_copy(side, i).start()

    total_tap = taps[0]
    for t in range(1, 9):
        total_tap = total_tap + taps[t]
    total_vec = jnp.full((CH, LANES), total_tap, f32)
    tap = [jnp.full((CH, LANES), taps[t], f32) / total_vec for t in range(9)]

    def hops(way):
        return l + way * (nl - 1 - 2 * l)

    def sizes(n):
        m = lax.rem(n, 4)
        return ((CH, m == 3), (2 * CH, m == 0), (CH + CH // 2, (m == 1) | (m == 2)))

    def main_copy(way, i, size):
        return pltpu.make_async_remote_copy(
            src_ref=outbox.at[way, i, pl.ds(0, size), :],
            dst_ref=inbox.at[way, i - lax.rem(hops(way), 2), pl.ds(0, size), :],
            send_sem=s_main.at[way, i],
            recv_sem=r_main.at[way, i - lax.rem(hops(way), 2)],
            device_id=(l + 1 - 2 * way, d),
            device_id_type=MESH,
        )

    def side_copy(way, side, i):
        return pltpu.make_async_remote_copy(
            src_ref=side_out.at[way, side, i],
            dst_ref=side_in.at[way, 1 - side, i - 1],
            send_sem=s_nb.at[way, side, i],
            recv_sem=r_nb.at[way, 1 - side, i - 1],
            device_id=(l + 1 - 2 * way, d - 1 + 2 * side),
            device_id_type=MESH,
        )

    def wait_recv(dst, sem):
        pltpu.make_async_copy(dst, dst, sem).wait()

    def receive(way, i, lead):
        n = hops(way)
        odd = lax.rem(n, 2)
        base = pl.multiple_of(PAD + i * CH - 16 * odd, 16)
        rows = pl.ds(base, CH)

        early = (lax.rem(i, 2) == 0) & (i < 2 * NF)

        @pl.when(early & lead)
        def _():
            j = lax.div(i, 2)
            for side, there in sides:

                @pl.when(there)
                def _():
                    wait_recv(fade_in.at[side, j], r_fade.at[side, j])

            at = pl.multiple_of(PAD + i * CH, CH)
            for x in range(SL):
                lo = fade_in[0, j, x]
                hi = fade_in[1, j, x]
                fade_b[x, pl.ds(at, CH), :] = jnp.where(low_half, hi, pltpu.roll(lo, LANES // 2, 1))
                fade_b[x, pl.ds(at + CH, CH), :] = jnp.where(
                    low_half, pltpu.roll(hi, LANES // 2, 1), lo
                )

        for size, sent in sizes(n + 3):

            @pl.when((n > 0) & sent & (i < NCH - 1 + odd))
            def _():
                wait_recv(inbox.at[way, i, pl.ds(0, size), :], r_main.at[way, i])
                lev[way, 0, 0, rows, :] = inbox[way, i, 0:CH, :]
                if size == 2 * CH:
                    lev[way, 0, 1, rows, :] = inbox[way, i, CH : 2 * CH, :]
                elif size > CH:
                    near = inbox[way, i, CH:size, :]
                    lev[way, 0, 1, pl.ds(base, half_ch), :] = pltpu.roll(near, 96, 1)
                    lev[way, 0, 1, pl.ds(base + half_ch, half_ch), :] = pltpu.roll(near, 32, 1)

        @pl.when((lax.rem(n, 4) == 0) & (i < NCH - 1))
        def _():
            @pl.when(n == 0)
            def _():
                for side, there in sides:

                    @pl.when(there)
                    def _():
                        wait_recv(light_nb.at[way, side, rows, :], r_nb.at[way, side, i])

                lev[way, 0, 1, rows, :] = jnp.where(
                    low_half, light_nb[way, 1, rows, :], light_nb[way, 0, rows, :]
                )

            @pl.when(n > 0)
            def _():
                for side, there in sides:

                    @pl.when(there)
                    def _():
                        wait_recv(side_in.at[way, side, i], r_nb.at[way, side, i])

                lo = side_in[way, 0, i]
                hi = side_in[way, 1, i]
                low = low_half[0:half_ch]
                lev[way, 0, 1, pl.ds(base, half_ch), :] = jnp.where(
                    low, hi, pltpu.roll(lo, LANES // 2, 1)
                )
                lev[way, 0, 1, pl.ds(base + half_ch, half_ch), :] = jnp.where(
                    low, pltpu.roll(hi, LANES // 2, 1), lo
                )

    def added(terms):
        while len(terms) > 1:
            terms = [sum(terms[j + 1 : j + 2], terms[j]) for j in range(0, len(terms), 2)]
        return terms[0]

    def slice_of(way, i, s):
        odd = lax.rem(hops(way), 2)
        base = pl.multiple_of(PAD + i * CH - 16 * odd, 16)
        layer = s + way * (SL - 1 - 2 * s)
        cols = []
        for tile in range(2):
            cols.append(
                added([tap[t] * lev[way, s, tile, pl.ds(base - 8 + t, CH), :] for t in range(9)])
            )
        a, b = cols
        sum_a, sum_b = tap[4] * a, tap[4] * b
        for t in range(9):
            by = t - 4
            if by == 0:
                continue
            ra = pltpu.roll(a, (-by) % LANES, 1)
            rb = pltpu.roll(b, (-by) % LANES, 1)
            own = lane < LANES - by if by > 0 else lane >= -by
            sum_a = sum_a + tap[t] * jnp.where(own, ra, rb)
            sum_b = sum_b + tap[t] * jnp.where(own, rb, ra)
        there_rows = pl.ds(base - 4 * (s + 1), CH)
        fade_far = fade_b[layer, there_rows, :]
        return sum_a * fade[layer, there_rows, :], sum_b * fade_far

    def work(*chunks):
        for s in range(SL):
            got = [slice_of(way, i, s) for way, i in chunks]
            if s < SL - 1:
                for (way, i), (new_a, new_b) in zip(chunks, got):
                    odd = lax.rem(hops(way), 2)
                    rows = pl.ds(pl.multiple_of(PAD + i * CH - 16 * odd, 16), CH)
                    lev[way, s + 1, 0, rows, :] = new_a
                    lev[way, s + 1, 1, rows, :] = new_b
        for (way, i), (last_a, last_b) in zip(chunks, got):
            send(way, i, last_a, last_b)

    def send(way, i, last_a, last_b):
        n = hops(way)
        odd = lax.rem(n, 2)
        for size, sent in sizes(n):

            @pl.when((n < nl - 1) & sent & (i >= odd))
            def _():
                outbox[way, i, 0:CH, :] = last_a
                low = low_half[0:half_ch]
                if size == 2 * CH:
                    outbox[way, i, CH : 2 * CH, :] = last_b
                elif size > CH:
                    outbox[way, i, CH:size, :] = jnp.where(
                        low, pltpu.roll(last_b[0:half_ch], 32, 1), pltpu.roll(last_b[half_ch:CH], 96, 1)
                    )
                main_copy(way, i, size).start()
                if size == CH:
                    top, bottom = last_a[0:half_ch], last_a[half_ch:CH]
                    side_out[way, 0, i] = jnp.where(low, top, pltpu.roll(bottom, LANES // 2, 1))
                    side_out[way, 1, i] = jnp.where(low, pltpu.roll(top, LANES // 2, 1), bottom)
                    for side, there in sides:

                        @pl.when(there)
                        def _():
                            side_copy(way, side, i).start()

    row_i = lax.broadcasted_iota(jnp.int32, (LANES, LANES), 0)
    lane_i = lax.broadcasted_iota(jnp.int32, (LANES, LANES), 1)

    def compact(column):
        return jnp.sum(jnp.where(row_i == lane_i, column, 0.0), axis=0, keepdims=True)

    def total_copy(j):
        peer = lax.rem(d + j, nd)
        return pltpu.make_async_remote_copy(
            src_ref=totals,
            dst_ref=gathered.at[d],
            send_sem=s_tot.at[j],
            recv_sem=r_tot.at[d],
            device_id=(l, peer),
            device_id_type=MESH,
        )

    def prepare():
        earlier = (row_i < lane_i).astype(f32)
        later = (row_i > lane_i).astype(f32)

        @pl.loop(0, BLOCKS)
        def _(b):
            x = lax.div(b, SL)
            at = pl.ds(pl.multiple_of(lax.rem(b, SL) * LANES, LANES), LANES)
            v = dens[x, at, :]
            tau = thick * channel(v, coef[3])
            front = jnp.dot(tau, earlier, precision=lax.Precision.HIGHEST, preferred_element_type=f32)
            back = jnp.dot(tau, later, precision=lax.Precision.HIGHEST, preferred_element_type=f32)
            flip = jnp.broadcast_to(flips[pl.ds(b, 1), :].astype(f32), (LANES, LANES)).T
            before = jnp.where(flip != 0.0, back, front)
            common = jnp.exp(-before) * (1.0 - jnp.exp(-tau))
            for k in range(3):
                weight[k, x, at, :] = common * channel(v, coef[k])
            totals[pl.ds(b, 1), :] = compact(jnp.sum(tau, axis=1, keepdims=True))

        @pl.loop(1, nd)
        def _(j):
            total_copy(j).start()

    def offsets():
        @pl.loop(1, nd)
        def _(j):
            peer = lax.rem(d + j, nd)
            wait_recv(gathered.at[peer], r_tot.at[peer])

        gathered[d] = totals[...]
        flip_px = flips[...] != 0
        offset = jnp.zeros((BLOCKS, LANES), f32)
        whole = jnp.zeros((BLOCKS, LANES), f32)
        for src in range(nd):
            got = gathered[src]
            whole = whole + got
            ahead = jnp.where(flip_px, src - d, d - src) > 0
            offset = offset + jnp.where(ahead, got, 0.0)
        through[...] = jnp.exp(-offset)
        alpha[...] = 1.0 - jnp.exp(-whole)

    def part_copy(peer):
        return pltpu.make_async_remote_copy(
            src_ref=part.at[peer, 0:4],
            dst_ref=parts.at[d, 0:4],
            send_sem=s_part.at[peer],
            recv_sem=r_part.at[d],
            device_id=(l, peer),
            device_id_type=MESH,
        )

    def finish(g):
        y = pl.multiple_of(g * LANES, LANES)
        for x in range(SL):
            b = x * (ROWS // LANES) + g
            z = SL - 1 - x
            fwd = lev[0, x, 0, pl.ds(PAD + 4 * x + y, LANES), :]
            bwd = lev[1, z, 0, pl.ds(PAD + 4 * z + y, LANES), :]
            lit = AMBIENT + fwd + bwd
            for k in range(3):
                s = jnp.sum(weight[k, x, pl.ds(y, LANES), :] * lit, axis=1, keepdims=True)
                part[b, k : k + 1, :] = compact(s) * through[pl.ds(b, 1), :]

            @pl.when(b != d)
            def _():
                part_copy(b).start()

    lead_way = (2 * l >= nl).astype(jnp.int32)
    n_lead = hops(lead_way)
    gap = jnp.where(2 * n_lead >= nl - 2, 8, NCH)
    prep_at = jnp.where(n_lead >= 4, 0, NCH)

    @pl.loop(0, 2 * NCH + 1)
    def _(item):
        @pl.when(item == prep_at)
        def _():
            prepare()

        @pl.when(item != prep_at)
        def _():
            k = item - (item > prep_at).astype(jnp.int32)
            e = k - gap
            first_on = k < NCH
            second_on = (e >= 0) & (e < NCH)

            @pl.when(e == 0)
            def _():
                offsets()

            @pl.when(first_on & second_on)
            def _():
                receive(lead_way, k, True)
                receive(1 - lead_way, e, False)
                work((lead_way, k), (1 - lead_way, e))

            @pl.when(first_on != second_on)
            def _():
                i = jnp.where(first_on, k, e)
                way = jnp.where(first_on, lead_way, 1 - lead_way)
                receive(way, i, first_on)
                work((way, i))

            @pl.when(second_on & (e > 0) & (lax.rem(e, 4) == 0))
            def _():
                finish(lax.div(e, 4) - 1)

    @pl.loop(1, nd)
    def _(j):
        peer = lax.rem(d + j, nd)
        wait_recv(parts.at[peer, 0:4], r_part.at[peer])

    parts[d] = part[d]
    image = parts[0]
    for src in range(1, nd):
        image = image + parts[src]
    out[0:3, :] = image[0:3, :]
    out[3:4, :] = alpha[pl.ds(d, 1), :]

    @pl.loop(1, nd)
    def _(j):
        total_copy(j).wait_send()
        part_copy(lax.rem(d + j, nd)).wait_send()

    for side, there in sides:

        @pl.when(there)
        def _():
            @pl.loop(0, NF)
            def _(i):
                fade_copy(side, i).wait_send()

    for way, first in ((0, 0), (1, nl - 1)):
        n = hops(way)
        odd = lax.rem(n, 2)

        @pl.loop(0, NCH)
        def _(i):
            for size, sent in sizes(n):

                @pl.when((n < nl - 1) & sent & (i >= odd))
                def _():
                    main_copy(way, i, size).wait_send()

            for side, there in sides:

                @pl.when(there & (n < nl - 1) & (lax.rem(n, 4) == 3) & (i >= odd))
                def _():
                    side_copy(way, side, i).wait_send()

                @pl.when(there & (l == first) & (i < NCH - 1))
                def _():
                    source_copy(way, side, i).wait_send()


def solution(mesh):
    nl, nd = mesh.shape["light"], mesh.shape["depth"]
    mine = BLOCKS // nd
    f32 = jnp.float32
    dma = pltpu.SemaphoreType.DMA

    def per_device(density, tf_table, tf_index, light_sources, spread_taps, view_flip):
        vmem = pl.BlockSpec(memory_space=pltpu.VMEM)
        anywhere = pl.BlockSpec(memory_space=pl.ANY)
        smem = pl.BlockSpec(memory_space=pltpu.SMEM)
        return pl.pallas_call(
            functools.partial(kernel, nl, nd),
            out_shape=jax.ShapeDtypeStruct((4, mine * LANES), f32),
            in_specs=[anywhere, smem, smem, anywhere, smem, vmem],
            out_specs=vmem,
            scratch_shapes=[
                pltpu.VMEM((SL, ROWS, LANES), f32),
                pltpu.VMEM((2, ROWS, LANES), f32),
                pltpu.VMEM((2, SL, 2, TALL, LANES), f32),
                pltpu.VMEM((2, NCH, 2 * CH, LANES), f32),
                pltpu.VMEM((2, NCH, 2 * CH, LANES), f32),
                pltpu.VMEM((2, 2, NCH, CH // 2, LANES), f32),
                pltpu.VMEM((2, 2, NCH, CH // 2, LANES), f32),
                pltpu.VMEM((SL, TALL, LANES), f32),
                pltpu.VMEM((SL, TALL, LANES), f32),
                pltpu.VMEM((2, NF, SL, CH, LANES), f32),
                pltpu.VMEM((2, NF, SL, CH, LANES), f32),
                pltpu.VMEM((2, 2, TALL, LANES), f32),
                pltpu.VMEM((3, SL, ROWS, LANES), f32),
                pltpu.VMEM((BLOCKS, LANES), f32),
                pltpu.VMEM((nd, BLOCKS, LANES), f32),
                pltpu.VMEM((BLOCKS, 8, LANES), f32),
                pltpu.VMEM((nd, 8, LANES), f32),
                pltpu.VMEM((BLOCKS, LANES), f32),
                pltpu.VMEM((BLOCKS, LANES), f32),
                dma((2, NCH)),
                dma((2, NCH)),
                dma((2, 2, NCH)),
                dma((2, 2, NCH)),
                dma((2, NF)),
                dma((2, NF)),
                dma((nd,)),
                dma((nd,)),
                dma((nd,)),
                dma((nd,)),
                dma((NF,)),
                dma((2,)),
            ],
            compiler_params=pltpu.CompilerParams(
                collective_id=0, has_side_effects=True, vmem_limit_bytes=48 << 20
            ),
            name="waves",
        )(density, tf_table, tf_index, light_sources, spread_taps, view_flip.reshape(BLOCKS, LANES))

    return jax.shard_map(
        per_device,
        mesh=mesh,
        in_specs=(
            P("light", None, "depth"),
            P(),
            P("light", "depth"),
            P(None, None, "depth"),
            P(),
            P("light"),
        ),
        out_specs=P(None, ("light", "depth")),
        check_vma=False,
    )
```
